32 devices in a mesh: row: 2 (over x), col: 16 (over z, y, core).
Axes of the slice: x: 2, y: 2, z: 4, core: 2. Of those that a mesh axis runs over, the one named last changes fastest.
Arguments:
- coords: float32 [64, 3, 256], P(('row', 'col')), may hold values from 0 to 8, as said below
- noise_var: float32 [64, 256], P(('row', 'col')), may hold values from 0.1 to 1
- right_side: float32 [64, 8, 256], P(('row', 'col')), may hold values from -32 to 32
- start_guess: float32 [64, 8, 256], P(('row', 'col')), may hold values from -3 to 3
- tile_pairs: int32 [2, 16, 2, 63], P('row', 'col'), may hold values from -1 to 31, as said below
Outputs:
- solution_field: float32 [64, 8, 256], P(('row', 'col'))
- residual: float32 [64, 8, 256], P(('row', 'col'))
The draws below stay inside these ranges and needn't reach their ends.
Inputs may be any that keep to these rules, and one draw needn't show every extreme that they name: `coords`: each tile's points lie within one unit cell of the integer lattice, and distinct tiles lie in distinct cells. `tile_pairs`: each device's list holds every pair of its block whose cells differ by at most one in each coordinate, each pair once and no other; listed entries come first, then entries of -1 in both rows.
All inputs are finite; a program needn't handle non-finite values.
Results may differ from the reference program's by a relative error of at most 0.0003.
Values sent between devices are 32-bit elements; how exact they have to be, the bound alone decides.
A program may use at most 64 MiB of HBM per device.

```python
import math
import jax
import jax.numpy as jnp
from jax import lax

TILE = 256
TPP = 2
RHS = 8
ITERS = 3
TILES = 64
TMAX = 63
N_ROW = 2
N_COL = 16


def lattice_cells(key):
    key_x, key_y = jax.random.split(jax.random.fold_in(key, 7))
    offset_row = jax.random.randint(key_x, (), 0, N_ROW)
    offset_col = jax.random.randint(key_y, (), 0, N_COL)
    tiles = jnp.arange(TILES, dtype=jnp.int32)
    pieces = tiles // TPP
    within = tiles % TPP
    row_index = pieces // N_COL
    col_index = pieces % N_COL
    half_rows = N_ROW // 2
    shifted_row = (row_index + offset_row) % N_ROW
    box_x = shifted_row // half_rows
    box_y = shifted_row % half_rows
    depth = N_COL // 8
    half_cols = N_COL // 2
    place = (col_index + offset_col) % N_COL
    local_x = place // half_cols
    step = place % half_cols
    local_y = step // depth
    lane = step % depth
    local_z = jnp.where(local_y % 2 == 0, lane, depth - 1 - lane)
    local_x = local_x + 2 * within
    local_y = (local_y + 2 * within) % 4
    local_z = (local_z + depth // 2 * within) % depth
    cell_x = 4 * box_x + local_x
    cell_y = 4 * box_y + local_y
    return jnp.stack([cell_x, cell_y, local_z], axis=1).astype(jnp.int32)


def draw_coords(key, part):
    cells = lattice_cells(key)
    fraction = jax.random.uniform(jax.random.fold_in(key, 11), (TILES, 3, TILE), jnp.float32)
    return cells[:, :, None].astype(jnp.float32) + fraction


def draw_tile_pairs(key, part):
    cells = lattice_cells(key)
    row_block = TPP * N_COL
    col_block = TPP * N_ROW
    row_ids = jnp.arange(N_ROW, dtype=jnp.int32)[:, None] * row_block + jnp.arange(row_block, dtype=jnp.int32)[None, :]
    col_local = jnp.arange(col_block, dtype=jnp.int32)[None, :]
    col_ids = (col_local // TPP * N_COL + jnp.arange(N_COL, dtype=jnp.int32)[:, None]) * TPP + col_local % TPP
    row_cells = cells[row_ids]
    col_cells = cells[col_ids]
    spacing = jnp.abs(row_cells[:, None, :, None, :] - col_cells[None, :, None, :, :])
    touching = jnp.all(spacing <= 1, axis=-1).astype(jnp.int32)
    flat = touching.reshape(N_ROW, N_COL, row_block * col_block)
    scores = jax.random.permutation(jax.random.fold_in(key, 13), row_block * col_block).astype(jnp.int32)
    ranking = (1 - flat) * (row_block * col_block) + scores[None, None, :]
    sorted_index = jnp.argsort(ranking, axis=-1, stable=True)[:, :, :TMAX].astype(jnp.int32)
    listed = jnp.take_along_axis(flat, sorted_index, axis=-1)
    row_tiles = jnp.where(listed > 0, sorted_index // col_block, -1)
    col_tiles = jnp.where(listed > 0, sorted_index % col_block, -1)
    return jnp.stack([row_tiles, col_tiles], axis=2).astype(jnp.int32)


def draw_right_side(key, part):
    key_values = jax.random.fold_in(jax.random.fold_in(key, 17), 0)
    key_column = jax.random.fold_in(jax.random.fold_in(key, 17), 2)
    position = jnp.arange(TILES, dtype=jnp.float32) / (TILES - 1)
    column_scale = 0.5 * 4.0 ** jax.random.uniform(key_column, (RHS,), jnp.float32)
    point_scale = 0.4 * 10.0 ** position
    values = jnp.clip(jax.random.normal(key_values, (TILES, RHS, TILE), jnp.float32), -4.0, 4.0)
    return values * point_scale[:, None, None] * column_scale[None, :, None]


def levels(rng, dims, cuts, low, top_value):
    factor_of = 1.0
    for dim, parts in cuts:
        heights = jax.random.uniform(jax.random.fold_in(jax.random.fold_in(rng, 6), dim), (parts,), jnp.float32, low / len(cuts), top_value / len(cuts))
        factor_of = factor_of * jnp.repeat(jnp.exp(heights), dims[dim] // parts).reshape((-1,) + (1,) * (len(dims) - 1 - dim))
    return factor_of


def normal_values(stream_key, extent, spread, bound, cuts=(), held_as=jnp.bfloat16):
    gain = levels(stream_key, extent, cuts, -0.22, 0.18) if cuts else 1.0
    result = jax.random.normal(stream_key, extent, jnp.float32) * spread * gain
    return jnp.minimum(jnp.maximum(result, -bound), bound).astype(held_as)


def setup_inputs(seed: int = 0) -> dict:
    streams_of = jax.random.split(jax.random.key(seed), 6)
    coords = draw_coords(jax.random.fold_in(streams_of[5], 71), 0)
    noise_var = jnp.clip(jnp.exp(math.log(1.0) - 2.3025851 * jax.random.uniform(streams_of[1], (TILES, TILE), jnp.float32) ** levels(streams_of[1], (TILES, TILE), ((0, 32),), -0.2, 0.2)), 0.1, 1.0)
    right_side = draw_right_side(jax.random.fold_in(streams_of[5], 71), 0)
    start_guess = normal_values(streams_of[3], (TILES, RHS, TILE), 0.5, 3.0, ((0, 32),), jnp.float32)
    tile_pairs = draw_tile_pairs(jax.random.fold_in(streams_of[5], 71), 0)
    return {"coords": coords, "noise_var": noise_var, "right_side": right_side, "start_guess": start_guess, "tile_pairs": tile_pairs}


def wendland(left_points, right_points):
    squared = jnp.zeros((left_points.shape[0], left_points.shape[2], right_points.shape[2]), jnp.float32)
    for component in range(3):
        spacing = left_points[:, component, :, None] - right_points[:, component, None, :]
        squared = squared + spacing * spacing
    distance = jnp.sqrt(squared)
    remain = jnp.maximum(1.0 - distance, 0.0)
    return remain ** 4 * (4.0 * distance + 1.0)

def global_pairs(tile_pairs):
    rows_local = tile_pairs[:, :, 0, :]
    cols_local = tile_pairs[:, :, 1, :]
    usable = rows_local >= 0
    row_grid = jnp.arange(N_ROW, dtype=jnp.int32)[:, None, None]
    col_grid = jnp.arange(N_COL, dtype=jnp.int32)[None, :, None]
    row_tiles = row_grid * (TPP * N_COL) + jnp.maximum(rows_local, 0)
    safe_cols = jnp.maximum(cols_local, 0)
    col_tiles = (safe_cols // TPP * N_COL + col_grid) * TPP + safe_cols % TPP
    total_pairs = N_ROW * N_COL * TMAX
    extra = -total_pairs % 64
    row_tiles = jnp.pad(row_tiles.reshape(-1), (0, extra)).astype(jnp.int32).reshape(-1, 64)
    col_tiles = jnp.pad(col_tiles.reshape(-1), (0, extra)).astype(jnp.int32).reshape(-1, 64)
    usable = jnp.pad(usable.reshape(-1), (0, extra)).reshape(-1, 64)
    return (row_tiles, col_tiles, usable)

def apply_operator(vectors, coords, noise_var, pairs):

    def accumulate(totals, group):
        rows_group, cols_group, use_group = group
        weights = wendland(coords[rows_group], coords[cols_group]) * use_group[:, None, None].astype(jnp.float32)
        product = jnp.einsum('pab,psb->psa', weights, vectors[cols_group], precision=lax.Precision.HIGHEST)
        return (totals.at[rows_group].add(product), None)
    totals, ignored = lax.scan(accumulate, jnp.zeros_like(vectors), pairs)
    return totals + noise_var[:, None, :] * vectors

def reference(coords, noise_var, right_side, start_guess, tile_pairs):
    pairs = global_pairs(tile_pairs)
    solution_field = start_guess
    residual = right_side - apply_operator(start_guess, coords, noise_var, pairs)
    direction = residual
    norm_now = lax.optimization_barrier(jnp.sum(residual * residual, axis=(0, 2)))
    for iteration in range(ITERS):
        applied = apply_operator(direction, coords, noise_var, pairs)
        step_size = norm_now / lax.optimization_barrier(jnp.sum(direction * applied, axis=(0, 2)))
        solution_field = solution_field + step_size[None, :, None] * direction
        residual = residual - step_size[None, :, None] * applied
        norm_next = lax.optimization_barrier(jnp.sum(residual * residual, axis=(0, 2)))
        direction = residual + (norm_next / norm_now)[None, :, None] * direction
        norm_now = norm_next
    return (solution_field, residual)
```

```python
import functools

import jax
import jax.numpy as jnp
from jax import lax
from jax.experimental import pallas as pl
from jax.experimental.pallas import tpu as pltpu
from jax.sharding import PartitionSpec as P

ITERS = 3
GROUP = 4
NEAR = 27
CAPACITY = -(-NEAR // GROUP) * GROUP
CORES = 2
MESH = pl.DeviceIdType.MESH
VMEM_SPEC = pl.BlockSpec(memory_space=pltpu.VMEM)
SMEM_SPEC = pl.BlockSpec(memory_space=pltpu.SMEM)
ANY_SPEC = pl.BlockSpec(memory_space=pl.ANY)


def factors(mesh_shape):
    rows, cols = mesh_shape
    chips = cols // CORES
    wide = 1
    while wide * wide * 4 <= chips:
        wide *= 2
    return rows, chips // wide, wide, CORES


def position(dims):
    xs, zs, ys, cs = dims
    x = lax.axis_index("row")
    col = lax.axis_index("col")
    return x, col // (ys * cs), (col // cs) % ys, col % cs


def flip(index, k, size):
    if size & (size - 1):
        return (k - index + 2 * size) % size
    result, bit = 0, 1
    while bit < size:
        result = result + (index // bit + k // bit) % 2 * bit
        bit *= 2
    return result


def gather_partners(dims):
    xs, zs, ys, cs = dims
    x, z, y, c = position(dims)
    partners = [(x, (((z + k) % zs) * ys + y) * cs + c) for k in range(1, zs)]
    if xs == 2 and ys == 2:
        partners += [(1 - x, (z * ys + 1 - y) * cs + c)]
    partners += [(x, (z * ys + (y + k) % ys) * cs + c) for k in range(1, ys)]
    partners += [((x + k) % xs, (z * ys + y) * cs + c) for k in range(1, xs)]
    partners += [(x, (z * ys + y) * cs + 1 - c)]
    return partners


def gather(dims, ins, outs, send_sem, recv_sem, local_sem):
    xs, zs, ys, cs = dims
    count = len(ins)
    x, z, y, c = position(dims)

    def device(xx, zz, yy, cc):
        return (xx, (zz * ys + yy) * cs + cc)

    def slot(xx, zz, yy, cc):
        return ((xx * zs + zz) * ys + yy) * cs + cc

    local = []
    for a in range(count):
        copy = pltpu.make_async_copy(ins[a], outs[a].at[slot(x, z, y, c)], local_sem.at[a])
        copy.start()
        local.append(copy)

    numbers = iter(range(10**6))
    sent = []

    def send(a, source, place, target):
        number = next(numbers)
        copy = pltpu.make_async_remote_copy(
            src_ref=source,
            dst_ref=outs[a].at[place],
            send_sem=send_sem.at[number],
            recv_sem=recv_sem.at[number],
            device_id=target,
            device_id_type=MESH,
        )
        copy.start()
        sent.append(copy)
        return copy

    mine = slot(x, z, y, c)
    other = device(x, z, y, 1 - c)
    along_z = {}
    for k in reversed(range(1, zs)):
        for a in range(count):
            along_z[k, a] = send(a, ins[a], mine, device(x, flip(z, k, zs), y, c))
    if xs == 2 and ys == 2:
        across_by = ((1 - x, 1 - y), ((x + c) % 2, (y + 1 - c) % 2), ((x + 1 - c) % 2, (y + c) % 2))
        arrivals, swaps = [], []

        def hand_on(k):
            level = flip(z, k, zs)
            for a in range(count):
                if k:
                    along_z[k, a].wait_recv()
                place = slot(x, level, y, c)
                source = outs[a].at[place] if k else ins[a]
                for xx, yy in across_by:
                    copy = send(a, source, place, device(xx, z, yy, c))
                    arrivals.append((copy, a, slot(xx, level, yy, c)))
                swaps.append(send(a, source, place, other))

        hand_on(0)
        yield
        for k in range(1, zs):
            hand_on(k)
        for way in (1, 2, 0):
            for copy, a, place in arrivals[way::3]:
                copy.wait_recv()
                swaps.append(send(a, outs[a].at[place], place, other))
        for copy in swaps:
            copy.wait_recv()
        for copy in sent:
            copy.wait_send()
        for copy in local:
            copy.wait()
        return

    yield
    for copy in local:
        copy.wait()

    def across(places, targets):
        for place in places:
            for a in range(count):
                for target in targets:
                    send(a, outs[a].at[place], place, target)

    def settle():
        for copy in sent:
            copy.wait()
        del sent[:]

    settle()
    across(
        [slot(x, zz, y, c) for zz in range(zs)],
        [device(x, z, (y + k) % ys, c) for k in range(1, ys)],
    )
    settle()
    across(
        [slot(x, zz, yy, c) for zz in range(zs) for yy in range(ys)],
        [device((x + k) % xs, z, y, c) for k in range(1, xs)],
    )
    settle()
    across(
        [slot(xx, zz, yy, c) for xx in range(xs) for zz in range(zs) for yy in range(ys)],
        [other],
    )
    settle()


def gather_kernel(dims, count, *refs):
    ins, outs = refs[:count], refs[count : 2 * count]
    send_sem, recv_sem, local_sem = refs[2 * count :]
    partners = gather_partners(dims)
    barrier = pltpu.get_barrier_semaphore()
    for partner in partners:
        pl.semaphore_signal(barrier, inc=1, device_id=partner, device_id_type=MESH)
    pl.semaphore_wait(barrier, len(partners))
    for _ in gather(dims, ins, outs, send_sem, recv_sem, local_sem):
        pass


def all_gather(dims, collective_id, *slabs):
    devices = dims[0] * dims[1] * dims[2] * dims[3]
    count = len(slabs)
    return pl.pallas_call(
        functools.partial(gather_kernel, dims, count),
        out_shape=[jax.ShapeDtypeStruct((devices,) + slab.shape, slab.dtype) for slab in slabs],
        in_specs=[VMEM_SPEC] * count,
        out_specs=[VMEM_SPEC] * count,
        scratch_shapes=[
            pltpu.SemaphoreType.DMA((count * (devices - 1),)),
            pltpu.SemaphoreType.DMA((count * (devices - 1),)),
            pltpu.SemaphoreType.DMA((count,)),
        ],
        compiler_params=pltpu.CompilerParams(collective_id=collective_id, has_side_effects=True),
    )(*slabs)


def split_rows(values):
    rest = values - values.astype(jnp.bfloat16).astype(jnp.float32)
    return jnp.concatenate([values, rest], axis=0).astype(jnp.bfloat16)


def solve_kernel(
    dims, groups,
    near_ref, side_ref, points_ref, own_points_ref, noise_ref, right_ref, guess_ref, guesses_ref,
    field_out, residual_out,
    buffer0, buffer1, buffer2, dir_ref, blocks, outgoing, dot_ref, dots_ref,
    send_sem, recv_sem, local_sem, dot_send, dot_recv,
):
    cols = dims[1] * dims[2] * dims[3]
    devices = dims[0] * cols
    tiles, tile = points_ref.shape[0], points_ref.shape[2]
    own, rhs, _ = right_ref.shape
    me = lax.axis_index("row") * cols + lax.axis_index("col")

    def peer(k):
        number = (me + k) % devices
        return (number // cols, number % cols)

    barrier = pltpu.get_barrier_semaphore()

    def greet(k, carry):
        pl.semaphore_signal(barrier, inc=1, device_id=peer(k), device_id_type=MESH)
        return carry

    lax.fori_loop(1, devices, greet, 0)

    def spreading(number, source):
        return gather(
            dims, [source], [(buffer0, buffer1, buffer2)[number]],
            send_sem.at[number], recv_sem.at[number], local_sem.at[number],
        )

    def spread(number, shadow=None):
        result = None
        for _ in spreading(number, outgoing.at[number]):
            if shadow is not None:
                result, shadow = shadow(), None
        return result

    rows = 32
    block = 2 * tile

    def build(e, carry):
        left = points_ref[jnp.maximum(near_ref[e], 0)].T
        right = own_points_ref[side_ref[e // GROUP]]
        reach = jnp.minimum(near_ref[e] + 1, 1).astype(jnp.float32)
        for chunk in range(tile // rows):
            squared = None
            for component in range(3):
                spacing = (
                    left[chunk * rows : (chunk + 1) * rows, component : component + 1]
                    - right[component : component + 1, :]
                )
                term = spacing * spacing
                squared = term if squared is None else squared + term
            distance = squared * lax.rsqrt(jnp.maximum(squared, 1e-30))
            remain = jnp.maximum(reach - distance, 0.0)
            remain = remain * remain
            weights = remain * remain * (4.0 * distance + 1.0)
            high = weights.astype(jnp.bfloat16)
            low = (weights - high.astype(jnp.float32)).astype(jnp.bfloat16)
            at = pl.multiple_of(e * block + chunk * rows, rows)
            blocks[pl.ds(at, rows), :] = high
            at = pl.multiple_of(e * block + tile + chunk * rows, rows)
            blocks[pl.ds(at, rows), :] = low
        return carry

    def image_of(fetch):
        def step(g, totals):
            parts = []
            for i in range(GROUP):
                near = jnp.maximum(near_ref[g * GROUP + i], 0)
                part = split_rows(fetch(near // own, near % own))
                parts += [part, part]
            first = pl.multiple_of(g * GROUP * block, GROUP * block)
            term = jnp.dot(
                jnp.concatenate(parts, axis=1),
                blocks[pl.ds(first, GROUP * block), :],
                preferred_element_type=jnp.float32,
            )
            place = side_ref[g].astype(jnp.float32)
            return tuple(
                total + term * jnp.maximum(1.0 - jnp.abs(place - float(p)), 0.0)
                for p, total in enumerate(totals)
            )

        start = tuple(jnp.zeros((2 * rhs, tile), jnp.float32) for _ in range(own))
        totals = lax.fori_loop(0, groups, step, start, unroll=4 if groups % 4 == 0 else 2)
        return [total[:rhs] + total[rhs:] for total in totals]

    def over_tiles(body, start):
        def one(i, carry):
            return body(i // own, i % own, carry)

        return lax.fori_loop(0, tiles, one, start, unroll=16)

    zero = jnp.zeros((rhs, tile), jnp.float32)
    noise = [noise_ref[p : p + 1, :] for p in range(own)]

    def over_sums(body, count):
        start = (zero,) * count
        return [jnp.sum(total, axis=1, keepdims=True) for total in over_tiles(body, start)]

    lax.fori_loop(0, groups * GROUP, build, 0, unroll=2)
    pl.semaphore_wait(barrier, devices - 1)

    for p, image in enumerate(image_of(lambda i, p: guesses_ref[i, p])):
        outgoing[0, p] = right_ref[p] - (image + noise[p] * guess_ref[p])
    spread(0)

    for p, image in enumerate(image_of(lambda i, p: buffer0[i, p])):
        outgoing[1, p] = image + noise[p] * outgoing[0, p]

    def norm_of_residual():
        def square(i, p, totals):
            value = buffer0[i, p]
            return (totals[0] + value * value,)

        return over_sums(square, 1)[0]

    norm0 = spread(1, norm_of_residual)

    for p, image in enumerate(image_of(lambda i, p: buffer1[i, p])):
        outgoing[2, p] = image + noise[p] * outgoing[1, p]

    def first_step():
        def dots(i, p, totals):
            return (totals[0] + buffer0[i, p] * buffer1[i, p],)

        step0 = norm0 / over_sums(dots, 1)[0]

        def descend(i, p, totals):
            value = buffer0[i, p] - step0 * buffer1[i, p]
            dir_ref[i, p] = value
            return (totals[0] + value * value,)

        norm1 = over_sums(descend, 1)[0]
        turn0 = norm1 / norm0

        def redirect(i, p, carry):
            value = dir_ref[i, p]
            dir_ref[i, p] = value + turn0 * buffer0[i, p]
            buffer0[i, p] = value
            return carry

        over_tiles(redirect, 0)
        return step0, norm1, turn0

    step0, norm1, turn0 = spread(2, first_step)
    grow0 = 1.0 + turn0

    def image1(i, p):
        return grow0 * buffer1[i, p] - step0 * buffer2[i, p]

    own_image1 = [grow0 * outgoing[1, p] - step0 * outgoing[2, p] for p in range(own)]
    own_residual1 = [outgoing[0, p] - step0 * outgoing[1, p] for p in range(own)]
    own_dir1 = [own_residual1[p] + turn0 * outgoing[0, p] for p in range(own)]
    images, totals = [], [zero] * 3
    for p, image in enumerate(image_of(image1)):
        image = image + noise[p] * own_image1[p]
        images.append(image)
        values = (own_residual1[p], own_image1[p], own_dir1[p])
        totals = [total + value * image for total, value in zip(totals, values)]
    lanes = lax.broadcasted_iota(jnp.int32, (rhs, 128), 1)
    eyes = [lanes == lax.broadcasted_iota(jnp.int32, (rhs, 128), 0) + n * rhs for n in range(3)]
    row = jnp.zeros((1, 128), jnp.float32)
    for eye, total in zip(eyes, totals):
        share = jnp.sum(total, axis=1, keepdims=True)
        row = row + jnp.sum(jnp.where(eye, share, 0.0), axis=0, keepdims=True)
    dot_ref[...] = row
    dots_ref[me] = row

    def dot_copy(k):
        return pltpu.make_async_remote_copy(
            src_ref=dot_ref,
            dst_ref=dots_ref.at[me],
            send_sem=dot_send.at[k],
            recv_sem=dot_recv.at[k],
            device_id=peer(k),
            device_id_type=MESH,
        )

    def start_dot(k, carry):
        dot_copy(k).start()
        return carry

    def wait_dot(k, carry):
        dot_copy(k).wait()
        return carry

    lax.fori_loop(1, devices, start_dot, 0)

    def second_dots(i, p, totals):
        direction = dir_ref[i, p]
        image = buffer1[i, p] - step0 * buffer2[i, p]
        return (
            totals[0] + direction * image1(i, p),
            totals[1] + direction * image,
        )

    dir_image1, dir_image = over_sums(second_dots, 2)
    step1 = norm1 / dir_image1

    def second_descend(i, p, totals):
        image = buffer1[i, p] - step0 * buffer2[i, p]
        turned = image1(i, p)
        value = buffer0[i, p] - step1 * turned
        return (
            totals[0] + value * value,
            totals[1] + value * image,
            totals[2] + value * turned,
        )

    norm2, next_image, next_image1 = over_sums(second_descend, 3)
    turn1 = norm2 / norm1
    known = next_image + turn1 * (next_image1 + dir_image + turn1 * dir_image1)
    fields, residuals, directions, applied = [], [], [], []
    for p in range(own):
        residual = own_residual1[p] - step1 * own_image1[p]
        fields.append(guess_ref[p] + step0 * outgoing[0, p] + step1 * own_dir1[p])
        residuals.append(residual)
        directions.append(residual + turn1 * own_dir1[p])
        applied.append(
            outgoing[1, p] - step0 * outgoing[2, p] - step1 * images[p] + turn1 * own_image1[p]
        )

    lax.fori_loop(1, devices, wait_dot, 0)
    sums = jnp.sum(dots_ref[...], axis=0)
    first, second, third = [
        jnp.sum(jnp.where(eye, sums, 0.0), axis=1, keepdims=True) for eye in eyes
    ]
    step2 = norm2 / (known - step1 * (first - step1 * second + turn1 * third))
    for p in range(own):
        field_out[p] = fields[p] + step2 * directions[p]
        residual_out[p] = residuals[p] - step2 * applied[p]


def solve(dims, groups, collective_id, *operands):
    devices = dims[0] * dims[1] * dims[2] * dims[3]
    points, right = operands[2], operands[5]
    tile = points.shape[2]
    own, rhs, _ = right.shape
    dma = pltpu.SemaphoreType.DMA
    phases = ITERS
    return pl.pallas_call(
        functools.partial(solve_kernel, dims, groups),
        out_shape=[jax.ShapeDtypeStruct(right.shape, jnp.float32)] * 2,
        in_specs=[SMEM_SPEC] * 2 + [VMEM_SPEC] * 6,
        out_specs=[VMEM_SPEC] * 2,
        scratch_shapes=[
            *[pltpu.VMEM((devices, own, rhs, tile), jnp.float32)] * (phases + 1),
            pltpu.VMEM((groups * GROUP * 2 * tile, tile), jnp.bfloat16),
            pltpu.VMEM((ITERS, own, rhs, tile), jnp.float32),
            pltpu.VMEM((1, 128), jnp.float32),
            pltpu.VMEM((devices, 1, 128), jnp.float32),
            dma((phases, devices - 1)),
            dma((phases, devices - 1)),
            dma((phases, 1)),
            dma((devices,)),
            dma((devices,)),
        ],
        compiler_params=pltpu.CompilerParams(
            collective_id=collective_id, has_side_effects=True, vmem_limit_bytes=60 * 2**20
        ),
    )(*operands)


def shards(mesh_shape, coords, noise_var, right_side, start_guess, tile_pairs):
    dims = factors(mesh_shape)
    devices = mesh_shape[0] * mesh_shape[1]
    own, _, tile = coords.shape
    tiles = own * devices
    me = lax.axis_index("row") * mesh_shape[1] + lax.axis_index("col")
    padded = jnp.pad(coords, ((0, 0), (0, 5), (0, 0)))
    points, guesses = all_gather(dims, 0, padded, start_guess)
    points = points.reshape(tiles, 8, tile)

    low, high = jnp.min(points, axis=2), jnp.max(points, axis=2)
    gap = jnp.maximum(low[None] - high[:, None], low[:, None] - high[None])
    near = jnp.all(gap < 1.0, axis=2).astype(jnp.int32)
    needed = -(-jnp.sum(near, axis=1) // GROUP)
    largest = jnp.max(jnp.sum(needed.reshape(devices, own), axis=1))
    own_near = lax.dynamic_slice_in_dim(near, me * own, own)
    own_needed = lax.dynamic_slice_in_dim(needed, me * own, own)
    ids = jnp.arange(tiles, dtype=jnp.int32)
    rank = jnp.sum(own_near[:, None, :] * (ids[None, None, :] < ids[None, :, None]), axis=2)
    places = jnp.arange(own, dtype=jnp.int32)
    first = jnp.sum(own_needed[None, :] * (places[None, :] < places[:, None]), axis=1)
    goal = jnp.where(own_near > 0, rank + first[:, None] * GROUP, -1)
    capacity = own * CAPACITY
    slots = jnp.arange(capacity, dtype=jnp.int32)
    hit = goal.reshape(1, own * tiles) == slots[:, None]
    known = jnp.tile(ids + 1, own)[None]
    near_ids = (jnp.sum(jnp.where(hit, known, 0), axis=1) - 1).astype(jnp.int32)
    group_ids = jnp.arange(capacity // GROUP, dtype=jnp.int32)
    side = jnp.sum(group_ids[:, None] >= first[None, 1:], axis=1).astype(jnp.int32)

    near_ids, side, largest = lax.optimization_barrier((near_ids, side, largest))
    operands = (near_ids, side, points, padded, noise_var, right_side, start_guess, guesses)
    small = own * 4
    return tuple(
        lax.cond(
            largest <= small,
            functools.partial(solve, dims, small, 1),
            functools.partial(solve, dims, capacity // GROUP, 2),
            *operands,
        )
    )


def solution(mesh):
    placed = (
        P(("row", "col"), None, None),
        P(("row", "col"), None),
        P(("row", "col"), None, None),
        P(("row", "col"), None, None),
        P("row", "col", None, None),
    )
    return jax.shard_map(
        functools.partial(shards, (mesh.shape["row"], mesh.shape["col"])),
        mesh=mesh,
        in_specs=placed,
        out_specs=(P(("row", "col"), None, None), P(("row", "col"), None, None)),
        check_vma=False,
    )
```

```python
import functools

import jax
import jax.numpy as jnp
from jax import lax
from jax.experimental import pallas as pl
from jax.experimental.pallas import tpu as pltpu
from jax.sharding import PartitionSpec as P

ITERS = 3
GROUP = 4
NEAR = 27
CAPACITY = -(-NEAR // GROUP) * GROUP
CORES = 2
MESH = pl.DeviceIdType.MESH
VMEM_SPEC = pl.BlockSpec(memory_space=pltpu.VMEM)
SMEM_SPEC = pl.BlockSpec(memory_space=pltpu.SMEM)
ANY_SPEC = pl.BlockSpec(memory_space=pl.ANY)


def factors(mesh_shape):
    rows, cols = mesh_shape
    chips = cols // CORES
    wide = 1
    while wide * wide * 4 <= chips:
        wide *= 2
    return rows, chips // wide, wide, CORES


def position(dims):
    xs, zs, ys, cs = dims
    x = lax.axis_index("row")
    col = lax.axis_index("col")
    return x, col // (ys * cs), (col // cs) % ys, col % cs


def flip(index, k, size):
    if size & (size - 1):
        return (k - index + 2 * size) % size
    result, bit = 0, 1
    while bit < size:
        result = result + (index // bit + k // bit) % 2 * bit
        bit *= 2
    return result


def gather_partners(dims):
    xs, zs, ys, cs = dims
    x, z, y, c = position(dims)
    partners = [(x, (((z + k) % zs) * ys + y) * cs + c) for k in range(1, zs)]
    if xs == 2 and ys == 2:
        partners += [(1 - x, (z * ys + 1 - y) * cs + c)]
    partners += [(x, (z * ys + (y + k) % ys) * cs + c) for k in range(1, ys)]
    partners += [((x + k) % xs, (z * ys + y) * cs + c) for k in range(1, xs)]
    partners += [(x, (z * ys + y) * cs + 1 - c)]
    return partners


def gather(dims, ins, outs, send_sem, recv_sem, local_sem):
    xs, zs, ys, cs = dims
    count = len(ins)
    x, z, y, c = position(dims)

    def device(xx, zz, yy, cc):
        return (xx, (zz * ys + yy) * cs + cc)

    def slot(xx, zz, yy, cc):
        return ((xx * zs + zz) * ys + yy) * cs + cc

    local = []
    for a in range(count):
        copy = pltpu.make_async_copy(ins[a], outs[a].at[slot(x, z, y, c)], local_sem.at[a])
        copy.start()
        local.append(copy)

    numbers = iter(range(10**6))
    sent = []

    def send(a, source, place, target):
        number = next(numbers)
        copy = pltpu.make_async_remote_copy(
            src_ref=source,
            dst_ref=outs[a].at[place],
            send_sem=send_sem.at[number],
            recv_sem=recv_sem.at[number],
            device_id=target,
            device_id_type=MESH,
        )
        copy.start()
        sent.append(copy)
        return copy

    mine = slot(x, z, y, c)
    other = device(x, z, y, 1 - c)
    along_z = {}
    for k in reversed(range(1, zs)):
        for a in range(count):
            along_z[k, a] = send(a, ins[a], mine, device(x, flip(z, k, zs), y, c))
    if xs == 2 and ys == 2:
        across_by = ((1 - x, 1 - y), ((x + c) % 2, (y + 1 - c) % 2), ((x + 1 - c) % 2, (y + c) % 2))
        arrivals, swaps = [], []

        def hand_on(k):
            level = flip(z, k, zs)
            for a in range(count):
                if k:
                    along_z[k, a].wait_recv()
                place = slot(x, level, y, c)
                source = outs[a].at[place] if k else ins[a]
                for xx, yy in across_by:
                    copy = send(a, source, place, device(xx, z, yy, c))
                    arrivals.append((copy, a, slot(xx, level, yy, c)))
                swaps.append((a, send(a, source, place, other)))

        hand_on(0)
        yield "sent"
        for k in range(1, zs):
            hand_on(k)
        for first in range(count):
            for way in (1, 2, 0):
                for copy, a, place in arrivals[way::3]:
                    if a == first:
                        copy.wait_recv()
                        swaps.append((a, send(a, outs[a].at[place], place, other)))
        for first in range(count):
            for a, copy in swaps:
                if a == first:
                    copy.wait_recv()
            local[first].wait()
            if first == 0:
                yield "whole"
        for copy in sent:
            copy.wait_send()
        return

    for copy in local:
        copy.wait()

    def across(places, targets):
        for place in places:
            for a in range(count):
                for target in targets:
                    send(a, outs[a].at[place], place, target)

    def settle():
        for copy in sent:
            copy.wait()
        del sent[:]

    settle()
    across(
        [slot(x, zz, y, c) for zz in range(zs)],
        [device(x, z, (y + k) % ys, c) for k in range(1, ys)],
    )
    settle()
    across(
        [slot(x, zz, yy, c) for zz in range(zs) for yy in range(ys)],
        [device((x + k) % xs, z, y, c) for k in range(1, xs)],
    )
    settle()
    across(
        [slot(xx, zz, yy, c) for xx in range(xs) for zz in range(zs) for yy in range(ys)],
        [other],
    )
    settle()
    yield "whole"


def column_of(matrix, lane):
    lanes = lax.broadcasted_iota(jnp.int32, matrix.shape, 1)
    return jnp.sum(jnp.where(lanes == lane, matrix, 0.0), axis=1, keepdims=True)


def list_near(own, devices, me, points_ref, ids_ref, side_ref, largest_ref):
    tiles = own * devices
    table = jnp.concatenate([points_ref[:, 4 * p + 3, :128] for p in range(own)], axis=0)
    across = table.T
    far = None
    for component in range(3):
        low, high = table[:, component : component + 1], table[:, component + 3 : component + 4]
        low_row, high_row = across[component : component + 1], across[component + 3 : component + 4]
        gap = jnp.maximum(low - high_row, low_row - high)
        far = gap if far is None else jnp.maximum(far, gap)
    near = jnp.where(far < 1.0, 1.0, 0.0)
    needed = jnp.ceil(jnp.sum(near, axis=1, keepdims=True) * (1.0 / GROUP))
    groups = sum(needed[p * devices : (p + 1) * devices] for p in range(own))
    largest_ref[0] = jnp.max(groups).astype(jnp.int32)

    rows = lax.broadcasted_iota(jnp.int32, (tiles, tiles), 0)
    earlier = rows > lax.broadcasted_iota(jnp.int32, (tiles, tiles), 1)
    rank = jnp.dot(
        jnp.where(earlier, 1.0, 0.0).astype(jnp.bfloat16),
        near.astype(jnp.bfloat16),
        preferred_element_type=jnp.float32,
    )
    slots = lax.broadcasted_iota(jnp.int32, (tiles, ids_ref.shape[1]), 1).astype(jnp.float32)
    place = lax.broadcasted_iota(jnp.int32, (tiles, 1), 0)
    tile_ids = (place % devices * own + place // devices + 1).astype(jnp.float32)
    group_ids = lax.broadcasted_iota(jnp.int32, side_ref.shape, 1).astype(jnp.float32)
    found, side = 0.0, jnp.zeros(side_ref.shape, jnp.float32)
    first = jnp.zeros((1, 1), jnp.float32)
    for p in range(own):
        lane = p * devices + me
        chosen = column_of(near, lane)
        goal = jnp.where(chosen > 0.0, column_of(rank, lane) + first * GROUP, -1.0)
        found = found + jnp.where(goal == slots, tile_ids, 0.0)
        if p:
            side = side + jnp.where(group_ids >= first, 1.0, 0.0)
        first = first + jnp.ceil(jnp.sum(chosen, axis=0, keepdims=True) * (1.0 / GROUP))
    ids_ref[...] = (jnp.sum(found, axis=0, keepdims=True) - 1.0).astype(jnp.int32)
    side_ref[...] = side.astype(jnp.int32)


def gather_kernel(dims, coords_ref, guess_ref, points_ref, guesses_ref, ids_ref, side_ref,
                  largest_ref, slab_ref, send_sem, recv_sem, local_sem):
    own = coords_ref.shape[1]
    cols = dims[1] * dims[2] * dims[3]
    devices = dims[0] * cols
    partners = gather_partners(dims)
    barrier = pltpu.get_barrier_semaphore()
    for partner in partners:
        pl.semaphore_signal(barrier, inc=1, device_id=partner, device_id_type=MESH)
    lanes = lax.broadcasted_iota(jnp.int32, (1, coords_ref.shape[2]), 1)
    for p in range(own):
        box = jnp.zeros(lanes.shape, jnp.float32)
        for component in range(3):
            row = coords_ref[component, p : p + 1, :]
            slab_ref[4 * p + component : 4 * p + component + 1, :] = row
            box = jnp.where(lanes == component, jnp.min(row, axis=1, keepdims=True), box)
            box = jnp.where(lanes == component + 3, jnp.max(row, axis=1, keepdims=True), box)
        slab_ref[4 * p + 3 : 4 * p + 4, :] = box
    pl.semaphore_wait(barrier, len(partners))
    ins, outs = [slab_ref, guess_ref], [points_ref, guesses_ref]
    me = lax.axis_index("row") * cols + lax.axis_index("col")
    for stage in gather(dims, ins, outs, send_sem, recv_sem, local_sem):
        if stage == "whole":
            list_near(own, devices, me, points_ref, ids_ref, side_ref, largest_ref)


def all_gather(dims, collective_id, coords, guess):
    devices = dims[0] * dims[1] * dims[2] * dims[3]
    _, own, tile = coords.shape
    wide = -(-own * CAPACITY // 128) * 128
    return pl.pallas_call(
        functools.partial(gather_kernel, dims),
        out_shape=[
            jax.ShapeDtypeStruct((devices, 4 * own, tile), jnp.float32),
            jax.ShapeDtypeStruct((devices,) + guess.shape, jnp.float32),
            jax.ShapeDtypeStruct((1, wide), jnp.int32),
            jax.ShapeDtypeStruct((1, wide), jnp.int32),
            jax.ShapeDtypeStruct((1,), jnp.int32),
        ],
        in_specs=[VMEM_SPEC] * 2,
        out_specs=[VMEM_SPEC] * 4 + [SMEM_SPEC],
        scratch_shapes=[
            pltpu.VMEM((4 * own, tile), jnp.float32),
            pltpu.SemaphoreType.DMA((2 * (devices - 1),)),
            pltpu.SemaphoreType.DMA((2 * (devices - 1),)),
            pltpu.SemaphoreType.DMA((2,)),
        ],
        compiler_params=pltpu.CompilerParams(collective_id=collective_id, has_side_effects=True),
    )(coords, guess)


def three_parts(value):
    parts = []
    for _ in range(3):
        part = value.astype(jnp.bfloat16).astype(jnp.float32)
        parts.append(part)
        value = value - part
    return parts


def split_rows(values):
    rest = values - values.astype(jnp.bfloat16).astype(jnp.float32)
    return jnp.concatenate([values, rest], axis=0).astype(jnp.bfloat16)


def solve_kernel(
    dims, groups,
    near_ref, side_ref, points_ref, noise_ref, right_ref, guess_ref, guesses_ref,
    field_out, residual_out,
    buffer0, buffer1, buffer2, dir_ref, blocks, own_side, centers, outgoing, dot_ref, dots_ref,
    send_sem, recv_sem, local_sem, dot_send, dot_recv,
):
    cols = dims[1] * dims[2] * dims[3]
    devices = dims[0] * cols
    own, rhs, tile = right_ref.shape
    tiles = own * devices
    me = lax.axis_index("row") * cols + lax.axis_index("col")

    def peer(k):
        number = (me + k) % devices
        return (number // cols, number % cols)

    barrier = pltpu.get_barrier_semaphore()

    def greet(k, carry):
        pl.semaphore_signal(barrier, inc=1, device_id=peer(k), device_id_type=MESH)
        return carry

    lax.fori_loop(1, devices, greet, 0)

    def spreading(number, source):
        return gather(
            dims, [source], [(buffer0, buffer1, buffer2)[number]],
            send_sem.at[number], recv_sem.at[number], local_sem.at[number],
        )

    def spread(number, shadow=None):
        result = None
        for stage in spreading(number, outgoing.at[number]):
            if shadow is not None and result is None:
                result, shadow = shadow(), None
        return result

    rows = 32
    block = 2 * tile
    line = lax.broadcasted_iota(jnp.int32, (8, tile), 0)
    blank = jnp.zeros((4, tile), jnp.float32)

    def place_points(device, p):
        slab = points_ref[device]
        points = slab[:4]
        for other in range(1, own):
            points = jnp.where(p == other, slab[4 * other : 4 * other + 4], points)
        return jnp.concatenate([points, blank], axis=0)

    for p in range(own):
        points = place_points(me, p)
        center = jnp.floor(jnp.min(points, axis=1, keepdims=True))
        points = jnp.where(line < 3, points - center, 0.0)
        squares = jnp.sum(points * points, axis=0, keepdims=True)
        value = jnp.where(line == 3, 16.0, jnp.where(line == 4, 16.0 * squares, -32.0 * points))
        one, two, three = three_parts(value)
        own_side[p] = jnp.concatenate([one, two, one, three, one, two], axis=0).astype(jnp.bfloat16)
        centers[p] = jnp.broadcast_to(center, (8, tile))

    def build(e, carry):
        near = jnp.maximum(near_ref[0, e], 0)
        p = side_ref[0, e // GROUP]
        reach = jnp.minimum(near_ref[0, e] + 1, 1).astype(jnp.float32) * 4.0
        points = jnp.where(line < 3, place_points(near // own, near % own) - centers[p], 0.0)
        squares = jnp.sum(points * points, axis=0, keepdims=True)
        value = jnp.where(line == 3, squares, jnp.where(line == 4, 1.0, points))
        one, two, three = three_parts(value)
        left = jnp.concatenate([one, one, two, one, three, two], axis=0).astype(jnp.bfloat16)
        squared = lax.dot_general(
            left, own_side[p], (((0,), (0,)), ((), ())), preferred_element_type=jnp.float32
        )
        for chunk in range(tile // rows):
            spacing = jnp.maximum(squared[chunk * rows : (chunk + 1) * rows], 1e-30)
            remain = jnp.maximum(reach - spacing * lax.rsqrt(spacing), 0.0)
            twice = remain * remain
            weights = twice * twice * (5.0 - remain)
            high = weights.astype(jnp.bfloat16)
            low = (weights - high.astype(jnp.float32)).astype(jnp.bfloat16)
            at = pl.multiple_of(e * block + chunk * rows, rows)
            blocks[pl.ds(at, rows), :] = high
            at = pl.multiple_of(e * block + tile + chunk * rows, rows)
            blocks[pl.ds(at, rows), :] = low
        return carry

    def image_of(fetch):
        def step(g, totals):
            parts = []
            for i in range(GROUP):
                near = jnp.maximum(near_ref[0, g * GROUP + i], 0)
                part = split_rows(fetch(near // own, near % own))
                parts += [part, part]
            first = pl.multiple_of(g * GROUP * block, GROUP * block)
            term = jnp.dot(
                jnp.concatenate(parts, axis=1),
                blocks[pl.ds(first, GROUP * block), :],
                preferred_element_type=jnp.float32,
            )
            place = side_ref[0, g].astype(jnp.float32)
            return tuple(
                total + term * jnp.maximum(1.0 - jnp.abs(place - float(p)), 0.0)
                for p, total in enumerate(totals)
            )

        start = tuple(jnp.zeros((2 * rhs, tile), jnp.float32) for _ in range(own))
        totals = lax.fori_loop(0, groups, step, start, unroll=4 if groups % 4 == 0 else 2)
        return [(total[:rhs] + total[rhs:]) * (1.0 / 256.0) for total in totals]

    def over_tiles(body, start):
        def one(i, carry):
            return body(i // own, i % own, carry)

        return lax.fori_loop(0, tiles, one, start, unroll=16)

    zero = jnp.zeros((rhs, tile), jnp.float32)
    noise = [noise_ref[p : p + 1, :] for p in range(own)]

    def over_sums(body, count):
        start = (zero,) * count
        return [jnp.sum(total, axis=1, keepdims=True) for total in over_tiles(body, start)]

    lax.fori_loop(0, groups * GROUP, build, 0, unroll=2)
    pl.semaphore_wait(barrier, devices - 1)

    for p, image in enumerate(image_of(lambda i, p: guesses_ref[i, p])):
        outgoing[0, p] = right_ref[p] - (image + noise[p] * guess_ref[p])
    spread(0)

    for p, image in enumerate(image_of(lambda i, p: buffer0[i, p])):
        outgoing[1, p] = image + noise[p] * outgoing[0, p]

    def norm_of_residual():
        def square(i, p, totals):
            value = buffer0[i, p]
            return (totals[0] + value * value,)

        return over_sums(square, 1)[0]

    norm0 = spread(1, norm_of_residual)

    for p, image in enumerate(image_of(lambda i, p: buffer1[i, p])):
        outgoing[2, p] = image + noise[p] * outgoing[1, p]

    def first_step():
        def dots(i, p, totals):
            return (totals[0] + buffer0[i, p] * buffer1[i, p],)

        step0 = norm0 / over_sums(dots, 1)[0]

        def descend(i, p, totals):
            value = buffer0[i, p] - step0 * buffer1[i, p]
            dir_ref[i, p] = value
            return (totals[0] + value * value,)

        norm1 = over_sums(descend, 1)[0]
        turn0 = norm1 / norm0

        def redirect(i, p, carry):
            value = dir_ref[i, p]
            dir_ref[i, p] = value + turn0 * buffer0[i, p]
            buffer0[i, p] = value
            return carry

        over_tiles(redirect, 0)
        return step0, norm1, turn0

    step0, norm1, turn0 = spread(2, first_step)
    grow0 = 1.0 + turn0

    def image1(i, p):
        return grow0 * buffer1[i, p] - step0 * buffer2[i, p]

    own_image1 = [grow0 * outgoing[1, p] - step0 * outgoing[2, p] for p in range(own)]
    own_residual1 = [outgoing[0, p] - step0 * outgoing[1, p] for p in range(own)]
    own_dir1 = [own_residual1[p] + turn0 * outgoing[0, p] for p in range(own)]
    images, totals = [], [zero] * 3
    for p, image in enumerate(image_of(image1)):
        image = image + noise[p] * own_image1[p]
        images.append(image)
        values = (own_residual1[p], own_image1[p], own_dir1[p])
        totals = [total + value * image for total, value in zip(totals, values)]
    lanes = lax.broadcasted_iota(jnp.int32, (rhs, 128), 1)
    eyes = [lanes == lax.broadcasted_iota(jnp.int32, (rhs, 128), 0) + n * rhs for n in range(3)]
    row = jnp.zeros((1, 128), jnp.float32)
    for eye, total in zip(eyes, totals):
        share = jnp.sum(total, axis=1, keepdims=True)
        row = row + jnp.sum(jnp.where(eye, share, 0.0), axis=0, keepdims=True)
    dot_ref[...] = row
    dots_ref[me] = row

    def dot_copy(k):
        return pltpu.make_async_remote_copy(
            src_ref=dot_ref,
            dst_ref=dots_ref.at[me],
            send_sem=dot_send.at[k],
            recv_sem=dot_recv.at[k],
            device_id=peer(k),
            device_id_type=MESH,
        )

    def start_dot(k, carry):
        dot_copy(k).start()
        return carry

    def wait_dot(k, carry):
        dot_copy(k).wait()
        return carry

    lax.fori_loop(1, devices, start_dot, 0)

    def second_dots(i, p, totals):
        direction = dir_ref[i, p]
        image = buffer1[i, p] - step0 * buffer2[i, p]
        return (
            totals[0] + direction * image1(i, p),
            totals[1] + direction * image,
        )

    dir_image1, dir_image = over_sums(second_dots, 2)
    step1 = norm1 / dir_image1

    def second_descend(i, p, totals):
        image = buffer1[i, p] - step0 * buffer2[i, p]
        turned = image1(i, p)
        value = buffer0[i, p] - step1 * turned
        return (
            totals[0] + value * value,
            totals[1] + value * image,
            totals[2] + value * turned,
        )

    norm2, next_image, next_image1 = over_sums(second_descend, 3)
    turn1 = norm2 / norm1
    known = next_image + turn1 * (next_image1 + dir_image + turn1 * dir_image1)
    fields, residuals, directions, applied = [], [], [], []
    for p in range(own):
        residual = own_residual1[p] - step1 * own_image1[p]
        fields.append(guess_ref[p] + step0 * outgoing[0, p] + step1 * own_dir1[p])
        residuals.append(residual)
        directions.append(residual + turn1 * own_dir1[p])
        applied.append(
            outgoing[1, p] - step0 * outgoing[2, p] - step1 * images[p] + turn1 * own_image1[p]
        )

    lax.fori_loop(1, devices, wait_dot, 0)
    sums = jnp.sum(dots_ref[...], axis=0)
    first, second, third = [
        jnp.sum(jnp.where(eye, sums, 0.0), axis=1, keepdims=True) for eye in eyes
    ]
    step2 = norm2 / (known - step1 * (first - step1 * second + turn1 * third))
    for p in range(own):
        field_out[p] = fields[p] + step2 * directions[p]
        residual_out[p] = residuals[p] - step2 * applied[p]


def solve(dims, groups, collective_id, *operands):
    devices = dims[0] * dims[1] * dims[2] * dims[3]
    right = operands[4]
    own, rhs, tile = right.shape
    dma = pltpu.SemaphoreType.DMA
    phases = ITERS
    return pl.pallas_call(
        functools.partial(solve_kernel, dims, groups),
        out_shape=[jax.ShapeDtypeStruct(right.shape, jnp.float32)] * 2,
        in_specs=[SMEM_SPEC] * 2 + [VMEM_SPEC] * 5,
        out_specs=[VMEM_SPEC] * 2,
        scratch_shapes=[
            *[pltpu.VMEM((devices, own, rhs, tile), jnp.float32)] * (phases + 1),
            pltpu.VMEM((groups * GROUP * 2 * tile, tile), jnp.bfloat16),
            pltpu.VMEM((own, 48, tile), jnp.bfloat16),
            pltpu.VMEM((own, 8, tile), jnp.float32),
            pltpu.VMEM((ITERS, own, rhs, tile), jnp.float32),
            pltpu.VMEM((1, 128), jnp.float32),
            pltpu.VMEM((devices, 1, 128), jnp.float32),
            dma((phases, devices - 1)),
            dma((phases, devices - 1)),
            dma((phases, 1)),
            dma((devices,)),
            dma((devices,)),
        ],
        compiler_params=pltpu.CompilerParams(
            collective_id=collective_id, has_side_effects=True, vmem_limit_bytes=60 * 2**20
        ),
    )(*operands)


def shards(mesh_shape, coords, noise_var, right_side, start_guess, tile_pairs):
    dims = factors(mesh_shape)
    own = coords.shape[0]
    placed = jnp.transpose(coords, (1, 0, 2))
    points, guesses, near_ids, side, largest = all_gather(dims, 0, placed, start_guess)
    operands = (near_ids, side, points, noise_var, right_side, start_guess, guesses)
    small = own * 4
    return tuple(
        lax.cond(
            largest[0] <= small,
            functools.partial(solve, dims, small, 1),
            functools.partial(solve, dims, own * CAPACITY // GROUP, 2),
            *operands,
        )
    )


def solution(mesh):
    placed = (
        P(("row", "col"), None, None),
        P(("row", "col"), None),
        P(("row", "col"), None, None),
        P(("row", "col"), None, None),
        P("row", "col", None, None),
    )
    return jax.shard_map(
        functools.partial(shards, (mesh.shape["row"], mesh.shape["col"])),
        mesh=mesh,
        in_specs=placed,
        out_specs=(P(("row", "col"), None, None), P(("row", "col"), None, None)),
        check_vma=False,
    )
```

```python
import functools

import jax
import jax.numpy as jnp
from jax import lax
from jax.experimental import pallas as pl
from jax.experimental.pallas import tpu as pltpu
from jax.sharding import PartitionSpec as P

ITERS = 3
GROUP = 4
NEAR = 27
CAPACITY = -(-NEAR // GROUP) * GROUP
CORES = 2
MESH = pl.DeviceIdType.MESH
VMEM_SPEC = pl.BlockSpec(memory_space=pltpu.VMEM)
SMEM_SPEC = pl.BlockSpec(memory_space=pltpu.SMEM)
ANY_SPEC = pl.BlockSpec(memory_space=pl.ANY)


def factors(mesh_shape):
    rows, cols = mesh_shape
    chips = cols // CORES
    wide = 1
    while wide * wide * 4 <= chips:
        wide *= 2
    return rows, chips // wide, wide, CORES


def position(dims):
    xs, zs, ys, cs = dims
    x = lax.axis_index("row")
    col = lax.axis_index("col")
    return x, col // (ys * cs), (col // cs) % ys, col % cs


def flip(index, k, size):
    if size & (size - 1):
        return (k - index + 2 * size) % size
    result, bit = 0, 1
    while bit < size:
        result = result + (index // bit + k // bit) % 2 * bit
        bit *= 2
    return result


def gather_partners(dims):
    xs, zs, ys, cs = dims
    x, z, y, c = position(dims)
    partners = [(x, (((z + k) % zs) * ys + y) * cs + c) for k in range(1, zs)]
    if xs == 2 and ys == 2:
        partners += [(1 - x, (z * ys + 1 - y) * cs + c)]
        partners += [(1 - x, (z * ys + yy) * cs + 1 - c) for yy in range(ys)]
        partners += [(x, (z * ys + 1 - y) * cs + 1 - c)]
    partners += [(x, (z * ys + (y + k) % ys) * cs + c) for k in range(1, ys)]
    partners += [((x + k) % xs, (z * ys + y) * cs + c) for k in range(1, xs)]
    partners += [(x, (z * ys + y) * cs + 1 - c)]
    return partners


def gather(dims, ins, outs, send_sem, recv_sem, local_sem):
    xs, zs, ys, cs = dims
    count = len(ins)
    x, z, y, c = position(dims)

    def device(xx, zz, yy, cc):
        return (xx, (zz * ys + yy) * cs + cc)

    def slot(xx, zz, yy, cc):
        return ((xx * zs + zz) * ys + yy) * cs + cc

    local = []
    for a in range(count):
        copy = pltpu.make_async_copy(ins[a], outs[a].at[slot(x, z, y, c)], local_sem.at[a])
        copy.start()
        local.append(copy)

    numbers = iter(range(10**6))
    sent = []

    def send(a, source, place, target):
        number = next(numbers)
        copy = pltpu.make_async_remote_copy(
            src_ref=source,
            dst_ref=outs[a].at[place],
            send_sem=send_sem.at[number],
            recv_sem=recv_sem.at[number],
            device_id=target,
            device_id_type=MESH,
        )
        copy.start()
        sent.append(copy)
        return copy

    mine = slot(x, z, y, c)
    other = device(x, z, y, 1 - c)
    along_z = {}
    for k in reversed(range(1, zs)):
        for a in range(count):
            along_z[k, a] = send(a, ins[a], mine, device(x, flip(z, k, zs), y, c))
    if xs == 2 and ys == 2:
        across_by = ((1 - x, 1 - y), ((x + c) % 2, (y + 1 - c) % 2), ((x + 1 - c) % 2, (y + c) % 2))
        arrivals, swaps = [], []

        def hand_on(k):
            level = flip(z, k, zs)
            for a in range(count):
                if k:
                    along_z[k, a].wait_recv()
                place = slot(x, level, y, c)
                source = outs[a].at[place] if k else ins[a]
                for xx, yy in across_by:
                    copy = send(a, source, place, device(xx, z, yy, c))
                    arrivals.append((copy, a, k, slot(xx, level, yy, c)))
                    if k == zs - 1:
                        swaps.append((a, send(a, source, place, device(xx, z, yy, 1 - c))))
                swaps.append((a, send(a, source, place, other)))

        hand_on(0)
        yield "sent"
        for k in range(1, zs):
            hand_on(k)
        for first in range(count):
            for way in (1, 2, 0):
                for copy, a, k, place in arrivals[way::3]:
                    if a == first and k < zs - 1:
                        copy.wait_recv()
                        swaps.append((a, send(a, outs[a].at[place], place, other)))
            for copy, a, k, place in arrivals:
                if a == first and k == zs - 1:
                    copy.wait_recv()
        for first in range(count):
            for a, copy in swaps:
                if a == first:
                    copy.wait_recv()
            local[first].wait()
            if first == 0:
                yield "whole"
        for copy in sent:
            copy.wait_send()
        return

    for copy in local:
        copy.wait()

    def across(places, targets):
        for place in places:
            for a in range(count):
                for target in targets:
                    send(a, outs[a].at[place], place, target)

    def settle():
        for copy in sent:
            copy.wait()
        del sent[:]

    settle()
    across(
        [slot(x, zz, y, c) for zz in range(zs)],
        [device(x, z, (y + k) % ys, c) for k in range(1, ys)],
    )
    settle()
    across(
        [slot(x, zz, yy, c) for zz in range(zs) for yy in range(ys)],
        [device((x + k) % xs, z, y, c) for k in range(1, xs)],
    )
    settle()
    across(
        [slot(xx, zz, yy, c) for xx in range(xs) for zz in range(zs) for yy in range(ys)],
        [other],
    )
    settle()
    yield "whole"


def column_of(matrix, lane):
    lanes = lax.broadcasted_iota(jnp.int32, matrix.shape, 1)
    return jnp.sum(jnp.where(lanes == lane, matrix, 0.0), axis=1, keepdims=True)


def list_near(own, devices, me, points_ref, ids_ref, side_ref, largest_ref):
    tiles = own * devices
    table = jnp.concatenate([points_ref[:, 4 * p + 3, :128] for p in range(own)], axis=0)
    across = table.T
    far = None
    for component in range(3):
        low, high = table[:, component : component + 1], table[:, component + 3 : component + 4]
        low_row, high_row = across[component : component + 1], across[component + 3 : component + 4]
        gap = jnp.maximum(low - high_row, low_row - high)
        far = gap if far is None else jnp.maximum(far, gap)
    near = jnp.where(far < 1.0, 1.0, 0.0)
    needed = jnp.ceil(jnp.sum(near, axis=1, keepdims=True) * (1.0 / GROUP))
    groups = sum(needed[p * devices : (p + 1) * devices] for p in range(own))
    largest_ref[0] = jnp.max(groups).astype(jnp.int32)

    rows = lax.broadcasted_iota(jnp.int32, (tiles, tiles), 0)
    earlier = rows > lax.broadcasted_iota(jnp.int32, (tiles, tiles), 1)
    rank = jnp.dot(
        jnp.where(earlier, 1.0, 0.0).astype(jnp.bfloat16),
        near.astype(jnp.bfloat16),
        preferred_element_type=jnp.float32,
    )
    slots = lax.broadcasted_iota(jnp.int32, (tiles, ids_ref.shape[1]), 1).astype(jnp.float32)
    place = lax.broadcasted_iota(jnp.int32, (tiles, 1), 0)
    tile_ids = (place % devices * own + place // devices + 1).astype(jnp.float32)
    group_ids = lax.broadcasted_iota(jnp.int32, side_ref.shape, 1).astype(jnp.float32)
    found, side = 0.0, jnp.zeros(side_ref.shape, jnp.float32)
    first = jnp.zeros((1, 1), jnp.float32)
    for p in range(own):
        lane = p * devices + me
        chosen = column_of(near, lane)
        goal = jnp.where(chosen > 0.0, column_of(rank, lane) + first * GROUP, -1.0)
        found = found + jnp.where(goal == slots, tile_ids, 0.0)
        if p:
            side = side + jnp.where(group_ids >= first, 1.0, 0.0)
        first = first + jnp.ceil(jnp.sum(chosen, axis=0, keepdims=True) * (1.0 / GROUP))
    ids_ref[...] = (jnp.sum(found, axis=0, keepdims=True) - 1.0).astype(jnp.int32)
    side_ref[...] = side.astype(jnp.int32)


def gather_kernel(dims, coords_in, guess_in, noise_in, points_ref, guesses_ref, noise_out, ids_ref, side_ref,
                  largest_ref, coords_ref, guess_ref, slab_ref, send_sem, recv_sem,
                  local_sem, fetch_sem):
    own = coords_ref.shape[1]
    cols = dims[1] * dims[2] * dims[3]
    devices = dims[0] * cols
    fetches = [
        pltpu.make_async_copy(coords_in, coords_ref, fetch_sem.at[0]),
        pltpu.make_async_copy(guess_in, guess_ref, fetch_sem.at[1]),
        pltpu.make_async_copy(noise_in, noise_out, fetch_sem.at[2]),
    ]
    for fetch in fetches:
        fetch.start()
    partners = gather_partners(dims)
    barrier = pltpu.get_barrier_semaphore()
    for partner in partners:
        pl.semaphore_signal(barrier, inc=1, device_id=partner, device_id_type=MESH)
    fetches[0].wait()
    lanes = lax.broadcasted_iota(jnp.int32, (1, coords_ref.shape[2]), 1)
    for p in range(own):
        box = jnp.zeros(lanes.shape, jnp.float32)
        for component in range(3):
            row = coords_ref[component, p : p + 1, :]
            slab_ref[4 * p + component : 4 * p + component + 1, :] = row
            box = jnp.where(lanes == component, jnp.min(row, axis=1, keepdims=True), box)
            box = jnp.where(lanes == component + 3, jnp.max(row, axis=1, keepdims=True), box)
        slab_ref[4 * p + 3 : 4 * p + 4, :] = box
    fetches[1].wait()
    pl.semaphore_wait(barrier, len(partners))
    ins, outs = [slab_ref, guess_ref], [points_ref, guesses_ref]
    me = lax.axis_index("row") * cols + lax.axis_index("col")
    for stage in gather(dims, ins, outs, send_sem, recv_sem, local_sem):
        if stage == "whole":
            list_near(own, devices, me, points_ref, ids_ref, side_ref, largest_ref)
    fetches[2].wait()


def all_gather(dims, collective_id, coords, guess, noise):
    devices = dims[0] * dims[1] * dims[2] * dims[3]
    _, own, tile = coords.shape
    wide = -(-own * CAPACITY // 128) * 128
    return pl.pallas_call(
        functools.partial(gather_kernel, dims),
        out_shape=[
            jax.ShapeDtypeStruct((devices, 4 * own, tile), jnp.float32),
            jax.ShapeDtypeStruct((devices,) + guess.shape, jnp.float32),
            jax.ShapeDtypeStruct(noise.shape, jnp.float32),
            jax.ShapeDtypeStruct((1, wide), jnp.int32),
            jax.ShapeDtypeStruct((1, wide), jnp.int32),
            jax.ShapeDtypeStruct((1,), jnp.int32),
        ],
        in_specs=[ANY_SPEC] * 3,
        out_specs=[VMEM_SPEC] * 5 + [SMEM_SPEC],
        scratch_shapes=[
            pltpu.VMEM(coords.shape, jnp.float32),
            pltpu.VMEM(guess.shape, jnp.float32),
            pltpu.VMEM((4 * own, tile), jnp.float32),
            pltpu.SemaphoreType.DMA((2 * (devices - 1),)),
            pltpu.SemaphoreType.DMA((2 * (devices - 1),)),
            pltpu.SemaphoreType.DMA((2,)),
            pltpu.SemaphoreType.DMA((3,)),
        ],
        compiler_params=pltpu.CompilerParams(collective_id=collective_id, has_side_effects=True),
    )(coords, guess, noise)


def three_parts(value):
    parts = []
    for _ in range(3):
        part = value.astype(jnp.bfloat16).astype(jnp.float32)
        parts.append(part)
        value = value - part
    return parts


def split_rows(values):
    rest = values - values.astype(jnp.bfloat16).astype(jnp.float32)
    return jnp.concatenate([values, rest], axis=0).astype(jnp.bfloat16)


def solve_kernel(
    dims, groups,
    near_ref, side_ref, points_ref, noise_ref, right_ref, guess_ref, guesses_ref,
    field_out, dir_out, residual_out, image_out, step_out,
    buffer0, buffer1, buffer2, dir_ref, blocks, own_side, centers, squared0, squared1, outgoing, dot_ref, dots_ref,
    send_sem, recv_sem, local_sem, dot_send, dot_recv,
):
    cols = dims[1] * dims[2] * dims[3]
    devices = dims[0] * cols
    own, rhs, tile = right_ref.shape
    tiles = own * devices
    me = lax.axis_index("row") * cols + lax.axis_index("col")

    def peer(k):
        number = (me + k) % devices
        return (number // cols, number % cols)

    barrier = pltpu.get_barrier_semaphore()

    def greet(k, carry):
        pl.semaphore_signal(barrier, inc=1, device_id=peer(k), device_id_type=MESH)
        return carry

    lax.fori_loop(1, devices, greet, 0)

    def spreading(number, source):
        return gather(
            dims, [source], [(buffer0, buffer1, buffer2)[number]],
            send_sem.at[number], recv_sem.at[number], local_sem.at[number],
        )

    def spread(number, shadow=None):
        result = None
        for stage in spreading(number, outgoing.at[number]):
            if shadow is not None and result is None:
                result, shadow = shadow(), None
        return result

    rows = 16
    block = 2 * tile
    line = lax.broadcasted_iota(jnp.int32, (8, tile), 0)
    blank = jnp.zeros((4, tile), jnp.float32)

    def place_points(device, p):
        slab = points_ref[device]
        points = slab[:4]
        for other in range(1, own):
            points = jnp.where(p == other, slab[4 * other : 4 * other + 4], points)
        return jnp.concatenate([points, blank], axis=0)

    for p in range(own):
        points = place_points(me, p)
        center = jnp.floor(jnp.min(points, axis=1, keepdims=True))
        points = jnp.where(line < 3, points - center, 0.0)
        squares = jnp.sum(points * points, axis=0, keepdims=True)
        value = jnp.where(line == 3, 16.0, jnp.where(line == 4, 16.0 * squares, -32.0 * points))
        one, two, three = three_parts(value)
        own_side[p] = jnp.concatenate([one, two, one, three, one, two], axis=0).astype(jnp.bfloat16)
        centers[p] = jnp.broadcast_to(center, (8, tile))

    def measure(e, target):
        near = jnp.maximum(near_ref[0, e], 0)
        p = side_ref[0, e // GROUP]
        points = jnp.where(line < 3, place_points(near // own, near % own) - centers[p], 0.0)
        squares = jnp.sum(points * points, axis=0, keepdims=True)
        value = jnp.where(line == 3, squares, jnp.where(line == 4, 1.0, points))
        one, two, three = three_parts(value)
        left = jnp.concatenate([one, one, two, one, three, two], axis=0).astype(jnp.bfloat16)
        target[...] = lax.dot_general(
            left, own_side[p], (((0,), (0,)), ((), ())), preferred_element_type=jnp.float32
        )

    def weigh(e, source):
        reach = jnp.minimum(near_ref[0, e] + 1, 1).astype(jnp.float32) * 4.0
        for chunk in range(tile // rows):
            spacing = jnp.maximum(source[chunk * rows : (chunk + 1) * rows], 1e-30)
            remain = jnp.maximum(reach - spacing * lax.rsqrt(spacing), 0.0)
            twice = remain * remain
            weights = twice * twice * (5.0 - remain)
            high = weights.astype(jnp.bfloat16)
            low = (weights - high.astype(jnp.float32)).astype(jnp.bfloat16)
            at = pl.multiple_of(e * block + chunk * rows, rows)
            blocks[pl.ds(at, rows), :] = high
            at = pl.multiple_of(e * block + tile + chunk * rows, rows)
            blocks[pl.ds(at, rows), :] = low

    def build(pair, carry):
        weigh(2 * pair, squared0)
        measure(2 * pair + 1, squared1)
        weigh(2 * pair + 1, squared1)
        measure(jnp.minimum(2 * pair + 2, groups * GROUP - 1), squared0)
        return carry

    def image_of(fetch):
        def step(g, totals):
            parts = []
            for i in range(GROUP):
                near = jnp.maximum(near_ref[0, g * GROUP + i], 0)
                part = split_rows(fetch(near // own, near % own))
                parts += [part, part]
            first = pl.multiple_of(g * GROUP * block, GROUP * block)
            term = jnp.dot(
                jnp.concatenate(parts, axis=1),
                blocks[pl.ds(first, GROUP * block), :],
                preferred_element_type=jnp.float32,
            )
            place = side_ref[0, g].astype(jnp.float32)
            return tuple(
                total + term * jnp.maximum(1.0 - jnp.abs(place - float(p)), 0.0)
                for p, total in enumerate(totals)
            )

        start = tuple(jnp.zeros((2 * rhs, tile), jnp.float32) for _ in range(own))
        totals = lax.fori_loop(0, groups, step, start, unroll=4 if groups % 4 == 0 else 2)
        return [(total[:rhs] + total[rhs:]) * (1.0 / 256.0) for total in totals]

    def over_tiles(body, start):
        def one(i, carry):
            return body(i // own, i % own, carry)

        return lax.fori_loop(0, tiles, one, start, unroll=16)

    zero = jnp.zeros((rhs, tile), jnp.float32)

    def over_sums(body, count):
        start = (zero,) * count
        return [jnp.sum(total, axis=1, keepdims=True) for total in over_tiles(body, start)]

    measure(0, squared0)
    lax.fori_loop(0, groups * GROUP // 2, build, 0, unroll=4)
    noise = [noise_ref[p : p + 1, :] for p in range(own)]
    pl.semaphore_wait(barrier, devices - 1)

    for p, image in enumerate(image_of(lambda i, p: guesses_ref[i, p])):
        outgoing[0, p] = right_ref[p] - (image + noise[p] * guess_ref[p])
    spread(0)

    for p, image in enumerate(image_of(lambda i, p: buffer0[i, p])):
        outgoing[1, p] = image + noise[p] * outgoing[0, p]

    def norm_of_residual():
        def square(i, p, totals):
            value = buffer0[i, p]
            return (totals[0] + value * value,)

        return over_sums(square, 1)[0]

    norm0 = spread(1, norm_of_residual)

    for p, image in enumerate(image_of(lambda i, p: buffer1[i, p])):
        outgoing[2, p] = image + noise[p] * outgoing[1, p]

    def first_step():
        def dots(i, p, totals):
            return (totals[0] + buffer0[i, p] * buffer1[i, p],)

        step0 = norm0 / over_sums(dots, 1)[0]

        def descend(i, p, totals):
            value = buffer0[i, p] - step0 * buffer1[i, p]
            dir_ref[i, p] = value
            return (totals[0] + value * value,)

        norm1 = over_sums(descend, 1)[0]
        turn0 = norm1 / norm0

        def redirect(i, p, carry):
            value = dir_ref[i, p]
            dir_ref[i, p] = value + turn0 * buffer0[i, p]
            buffer0[i, p] = value
            return carry

        over_tiles(redirect, 0)
        return step0, norm1, turn0

    step0, norm1, turn0 = spread(2, first_step)
    grow0 = 1.0 + turn0

    def image1(i, p):
        return grow0 * buffer1[i, p] - step0 * buffer2[i, p]

    own_image1 = [grow0 * outgoing[1, p] - step0 * outgoing[2, p] for p in range(own)]
    own_residual1 = [outgoing[0, p] - step0 * outgoing[1, p] for p in range(own)]
    own_dir1 = [own_residual1[p] + turn0 * outgoing[0, p] for p in range(own)]
    images, totals = [], [zero] * 3
    for p, image in enumerate(image_of(image1)):
        image = image + noise[p] * own_image1[p]
        images.append(image)
        values = (own_residual1[p], own_image1[p], own_dir1[p])
        totals = [total + value * image for total, value in zip(totals, values)]
    lanes = lax.broadcasted_iota(jnp.int32, (rhs, 128), 1)
    eyes = [lanes == lax.broadcasted_iota(jnp.int32, (rhs, 128), 0) + n * rhs for n in range(3)]
    row = jnp.zeros((1, 128), jnp.float32)
    for eye, total in zip(eyes, totals):
        share = jnp.sum(total, axis=1, keepdims=True)
        row = row + jnp.sum(jnp.where(eye, share, 0.0), axis=0, keepdims=True)
    dot_ref[...] = row
    dots_ref[me] = row

    def dot_copy(k):
        return pltpu.make_async_remote_copy(
            src_ref=dot_ref,
            dst_ref=dots_ref.at[me],
            send_sem=dot_send.at[k],
            recv_sem=dot_recv.at[k],
            device_id=peer(k),
            device_id_type=MESH,
        )

    def start_dot(k, carry):
        dot_copy(k).start()
        return carry

    def wait_dot(k, carry):
        dot_copy(k).wait()
        return carry

    lax.fori_loop(1, devices, start_dot, 0)

    def second_dots(i, p, totals):
        direction = dir_ref[i, p]
        image = buffer1[i, p] - step0 * buffer2[i, p]
        return (
            totals[0] + direction * image1(i, p),
            totals[1] + direction * image,
        )

    dir_image1, dir_image = over_sums(second_dots, 2)
    step1 = norm1 / dir_image1

    def second_descend(i, p, totals):
        image = buffer1[i, p] - step0 * buffer2[i, p]
        turned = image1(i, p)
        value = buffer0[i, p] - step1 * turned
        return (
            totals[0] + value * value,
            totals[1] + value * image,
            totals[2] + value * turned,
        )

    norm2, next_image, next_image1 = over_sums(second_descend, 3)
    turn1 = norm2 / norm1
    known = next_image + turn1 * (next_image1 + dir_image + turn1 * dir_image1)
    for p in range(own):
        residual = own_residual1[p] - step1 * own_image1[p]
        field_out[p] = guess_ref[p] + step0 * outgoing[0, p] + step1 * own_dir1[p]
        residual_out[p] = residual
        dir_out[p] = residual + turn1 * own_dir1[p]
        image_out[p] = (
            outgoing[1, p] - step0 * outgoing[2, p] - step1 * images[p] + turn1 * own_image1[p]
        )

    lax.fori_loop(1, devices, wait_dot, 0)
    sums = jnp.sum(dots_ref[...], axis=0)
    first, second, third = [
        jnp.sum(jnp.where(eye, sums, 0.0), axis=1, keepdims=True) for eye in eyes
    ]
    step2 = norm2 / (known - step1 * (first - step1 * second + turn1 * third))
    step_out[...] = jnp.broadcast_to(step2, (rhs, tile))


def solve(dims, groups, collective_id, *operands):
    devices = dims[0] * dims[1] * dims[2] * dims[3]
    right = operands[4]
    own, rhs, tile = right.shape
    dma = pltpu.SemaphoreType.DMA
    phases = ITERS
    return pl.pallas_call(
        functools.partial(solve_kernel, dims, groups),
        out_shape=[jax.ShapeDtypeStruct(right.shape, jnp.float32)] * 4
        + [jax.ShapeDtypeStruct((rhs, tile), jnp.float32)],
        in_specs=[SMEM_SPEC] * 2 + [VMEM_SPEC] * 5,
        out_specs=[VMEM_SPEC] * 5,
        scratch_shapes=[
            *[pltpu.VMEM((devices, own, rhs, tile), jnp.float32)] * (phases + 1),
            pltpu.VMEM((groups * GROUP * 2 * tile, tile), jnp.bfloat16),
            pltpu.VMEM((own, 48, tile), jnp.bfloat16),
            pltpu.VMEM((own, 8, tile), jnp.float32),
            *[pltpu.VMEM((tile, tile), jnp.float32)] * 2,
            pltpu.VMEM((ITERS, own, rhs, tile), jnp.float32),
            pltpu.VMEM((1, 128), jnp.float32),
            pltpu.VMEM((devices, 1, 128), jnp.float32),
            dma((phases, devices - 1)),
            dma((phases, devices - 1)),
            dma((phases, 1)),
            dma((devices,)),
            dma((devices,)),
        ],
        compiler_params=pltpu.CompilerParams(
            collective_id=collective_id, has_side_effects=True, vmem_limit_bytes=60 * 2**20
        ),
    )(*operands)


def shards(mesh_shape, coords, noise_var, right_side, start_guess, tile_pairs):
    dims = factors(mesh_shape)
    own = coords.shape[0]
    placed = jnp.transpose(coords, (1, 0, 2))
    gathered = all_gather(dims, 0, placed, start_guess, noise_var)
    points, guesses, noise, near_ids, side, largest = gathered
    operands = (near_ids, side, points, noise, right_side, start_guess, guesses)
    small = own * 4
    field, direction, residual, image, step = lax.cond(
        largest[0] <= small,
        functools.partial(solve, dims, small, 1),
        functools.partial(solve, dims, own * CAPACITY // GROUP, 2),
        *operands,
    )
    return field + step * direction, residual - step * image


def solution(mesh):
    placed = (
        P(("row", "col"), None, None),
        P(("row", "col"), None),
        P(("row", "col"), None, None),
        P(("row", "col"), None, None),
        P("row", "col", None, None),
    )
    return jax.shard_map(
        functools.partial(shards, (mesh.shape["row"], mesh.shape["col"])),
        mesh=mesh,
        in_specs=placed,
        out_specs=(P(("row", "col"), None, None), P(("row", "col"), None, None)),
        check_vma=False,
    )
```

```python
import functools

import jax
import jax.numpy as jnp
from jax import lax
from jax.experimental import pallas as pl
from jax.experimental.pallas import tpu as pltpu
from jax.sharding import PartitionSpec as P

ITERS = 3
GROUP = 4
NEAR = 27
CAPACITY = -(-NEAR // GROUP) * GROUP
CORES = 2
MESH = pl.DeviceIdType.MESH
VMEM_SPEC = pl.BlockSpec(memory_space=pltpu.VMEM)
SMEM_SPEC = pl.BlockSpec(memory_space=pltpu.SMEM)
ANY_SPEC = pl.BlockSpec(memory_space=pl.ANY)


def factors(mesh_shape):
    rows, cols = mesh_shape
    chips = cols // CORES
    wide = 1
    while wide * wide * 4 <= chips:
        wide *= 2
    return rows, chips // wide, wide, CORES


def position(dims):
    xs, zs, ys, cs = dims
    x = lax.axis_index("row")
    col = lax.axis_index("col")
    return x, col // (ys * cs), (col // cs) % ys, col % cs


def flip(index, k, size):
    if size & (size - 1):
        return (k - index + 2 * size) % size
    result, bit = 0, 1
    while bit < size:
        result = result + (index // bit + k // bit) % 2 * bit
        bit *= 2
    return result


def plane_order(x, y, c):
    return (1 - x, 1 - y), ((x + c) % 2, (y + 1 - c) % 2), ((x + 1 - c) % 2, (y + c) % 2)


def straight(k, levels, arrays):
    if arrays > 1 or k == 0 or k + 1 >= levels:
        return ()
    return (0, 1, 2)[: 3 if k == 1 else 1 if k == 2 else 0]


def gather_partners(dims):
    xs, zs, ys, cs = dims
    x, z, y, c = position(dims)
    partners = [(x, (((z + k) % zs) * ys + y) * cs + c) for k in range(1, zs)]
    if xs == 2 and ys == 2:
        partners += [(1 - x, (z * ys + 1 - y) * cs + c)]
        partners += [(1 - x, (z * ys + yy) * cs + 1 - c) for yy in range(ys)]
        partners += [(x, (z * ys + 1 - y) * cs + 1 - c)]
    partners += [(x, (z * ys + (y + k) % ys) * cs + c) for k in range(1, ys)]
    partners += [((x + k) % xs, (z * ys + y) * cs + c) for k in range(1, xs)]
    partners += [(x, (z * ys + y) * cs + 1 - c)]
    return partners


def gather(dims, ins, outs, send_sem, recv_sem, local_sem):
    xs, zs, ys, cs = dims
    count = len(ins)
    x, z, y, c = position(dims)

    def device(xx, zz, yy, cc):
        return (xx, (zz * ys + yy) * cs + cc)

    def slot(xx, zz, yy, cc):
        return ((xx * zs + zz) * ys + yy) * cs + cc

    local = []
    for a in range(count):
        copy = pltpu.make_async_copy(ins[a], outs[a].at[slot(x, z, y, c)], local_sem.at[a])
        copy.start()
        local.append(copy)

    numbers = iter(range(10**6))
    sent = []

    def send(a, source, place, target):
        number = next(numbers)
        copy = pltpu.make_async_remote_copy(
            src_ref=source,
            dst_ref=outs[a].at[place],
            send_sem=send_sem.at[number],
            recv_sem=recv_sem.at[number],
            device_id=target,
            device_id_type=MESH,
        )
        copy.start()
        sent.append(copy)
        return copy

    mine = slot(x, z, y, c)
    other = device(x, z, y, 1 - c)
    along_z = {}
    if xs == 2 and ys == 2:
        across_by = plane_order(x, y, c)
        last = zs - 1
        arrivals, swaps = {}, []

        def hand_on(k, a):
            level = flip(z, k, zs)
            if k:
                along_z[k, a].wait_recv()
            place = slot(x, level, y, c)
            source = outs[a].at[place] if k else ins[a]
            for way, (xx, yy) in enumerate(across_by):
                if way in straight(k, zs, count):
                    continue
                copy = send(a, source, place, device(xx, z, yy, c))
                arrivals[a, k, way] = (copy, slot(xx, level, yy, c))
                if k and k == last:
                    swaps.append((a, send(a, source, place, device(xx, z, yy, 1 - c))))
            swaps.append((a, send(a, source, place, other)))

        for k in reversed(range(1, zs)):
            for a in range(count):
                level = flip(z, k, zs)
                if k > 1:
                    along_z[k, a] = send(a, ins[a], mine, device(x, level, y, c))
                for way in straight(k, zs, count):
                    xx, yy = across_by[way]
                    copy = send(a, ins[a], mine, device(xx, level, yy, c))
                    arrivals[a, k, way] = (copy, slot(xx, level, yy, c))
                if k == 1:
                    along_z[k, a] = send(a, ins[a], mine, device(x, level, y, c))
        for a in range(count):
            hand_on(0, a)
        yield "sent"
        for k in sorted(range(1, zs), key=lambda k: (len(straight(k, zs, count)) == 3, k)):
            for a in range(count):
                hand_on(k, a)
        ways = (1, 2, 0)
        early = min(zs, 2) if count == 1 else 0
        order = [(k, way) for k in range(early) for way in ways]
        order += [(k, way) for way in ways for k in range(early, zs)]
        order.sort(key=lambda step: step[0] == last)
        for first in range(count):
            for k, way in order:
                copy, place = arrivals[first, k, way]
                copy.wait_recv()
                if k == 0 or k < last:
                    swaps.append((first, send(first, outs[first].at[place], place, other)))
        for first in range(count):
            for a, copy in swaps:
                if a == first:
                    copy.wait_recv()
            local[first].wait()
            if first == 0:
                yield "whole"
        for copy in sent:
            copy.wait_send()
        return

    for k in reversed(range(1, zs)):
        for a in range(count):
            along_z[k, a] = send(a, ins[a], mine, device(x, flip(z, k, zs), y, c))
    for copy in local:
        copy.wait()

    def across(places, targets):
        for place in places:
            for a in range(count):
                for target in targets:
                    send(a, outs[a].at[place], place, target)

    def settle():
        for copy in sent:
            copy.wait()
        del sent[:]

    settle()
    across(
        [slot(x, zz, y, c) for zz in range(zs)],
        [device(x, z, (y + k) % ys, c) for k in range(1, ys)],
    )
    settle()
    across(
        [slot(x, zz, yy, c) for zz in range(zs) for yy in range(ys)],
        [device((x + k) % xs, z, y, c) for k in range(1, xs)],
    )
    settle()
    across(
        [slot(xx, zz, yy, c) for xx in range(xs) for zz in range(zs) for yy in range(ys)],
        [other],
    )
    settle()
    yield "whole"


def column_of(matrix, lane):
    lanes = lax.broadcasted_iota(jnp.int32, matrix.shape, 1)
    return jnp.sum(jnp.where(lanes == lane, matrix, 0.0), axis=1, keepdims=True)


def list_near(own, devices, me, points_ref, ids_ref, side_ref, largest_ref):
    tiles = own * devices
    table = jnp.concatenate([points_ref[:, 4 * p + 3, :128] for p in range(own)], axis=0)
    across = table.T
    far = None
    for component in range(3):
        low, high = table[:, component : component + 1], table[:, component + 3 : component + 4]
        low_row, high_row = across[component : component + 1], across[component + 3 : component + 4]
        gap = jnp.maximum(low - high_row, low_row - high)
        far = gap if far is None else jnp.maximum(far, gap)
    near = jnp.where(far < 1.0, 1.0, 0.0)
    needed = jnp.ceil(jnp.sum(near, axis=1, keepdims=True) * (1.0 / GROUP))
    groups = sum(needed[p * devices : (p + 1) * devices] for p in range(own))
    largest_ref[0] = jnp.max(groups).astype(jnp.int32)

    rows = lax.broadcasted_iota(jnp.int32, (tiles, tiles), 0)
    earlier = rows > lax.broadcasted_iota(jnp.int32, (tiles, tiles), 1)
    rank = jnp.dot(
        jnp.where(earlier, 1.0, 0.0).astype(jnp.bfloat16),
        near.astype(jnp.bfloat16),
        preferred_element_type=jnp.float32,
    )
    slots = lax.broadcasted_iota(jnp.int32, (tiles, ids_ref.shape[1]), 1).astype(jnp.float32)
    place = lax.broadcasted_iota(jnp.int32, (tiles, 1), 0)
    tile_ids = (place % devices * own + place // devices + 1).astype(jnp.float32)
    group_ids = lax.broadcasted_iota(jnp.int32, side_ref.shape, 1).astype(jnp.float32)
    found, side = 0.0, jnp.zeros(side_ref.shape, jnp.float32)
    first = jnp.zeros((1, 1), jnp.float32)
    for p in range(own):
        lane = p * devices + me
        chosen = column_of(near, lane)
        goal = jnp.where(chosen > 0.0, column_of(rank, lane) + first * GROUP, -1.0)
        found = found + jnp.where(goal == slots, tile_ids, 0.0)
        if p:
            side = side + jnp.where(group_ids >= first, 1.0, 0.0)
        first = first + jnp.ceil(jnp.sum(chosen, axis=0, keepdims=True) * (1.0 / GROUP))
    ids_ref[...] = (jnp.sum(found, axis=0, keepdims=True) - 1.0).astype(jnp.int32)
    side_ref[...] = side.astype(jnp.int32)


def gather_kernel(dims, coords_in, guess_in, noise_in, points_ref, guesses_ref, noise_out, ids_ref, side_ref,
                  largest_ref, coords_ref, guess_ref, slab_ref, send_sem, recv_sem,
                  local_sem, fetch_sem):
    own = coords_ref.shape[1]
    cols = dims[1] * dims[2] * dims[3]
    devices = dims[0] * cols
    fetches = [
        pltpu.make_async_copy(coords_in, coords_ref, fetch_sem.at[0]),
        pltpu.make_async_copy(guess_in, guess_ref, fetch_sem.at[1]),
        pltpu.make_async_copy(noise_in, noise_out, fetch_sem.at[2]),
    ]
    for fetch in fetches:
        fetch.start()
    partners = gather_partners(dims)
    barrier = pltpu.get_barrier_semaphore()
    for partner in partners:
        pl.semaphore_signal(barrier, inc=1, device_id=partner, device_id_type=MESH)
    fetches[0].wait()
    lanes = lax.broadcasted_iota(jnp.int32, (1, coords_ref.shape[2]), 1)
    for p in range(own):
        box = jnp.zeros(lanes.shape, jnp.float32)
        for component in range(3):
            row = coords_ref[component, p : p + 1, :]
            slab_ref[4 * p + component : 4 * p + component + 1, :] = row
            box = jnp.where(lanes == component, jnp.min(row, axis=1, keepdims=True), box)
            box = jnp.where(lanes == component + 3, jnp.max(row, axis=1, keepdims=True), box)
        slab_ref[4 * p + 3 : 4 * p + 4, :] = box
    fetches[1].wait()
    pl.semaphore_wait(barrier, len(partners))
    ins, outs = [slab_ref, guess_ref], [points_ref, guesses_ref]
    me = lax.axis_index("row") * cols + lax.axis_index("col")
    for stage in gather(dims, ins, outs, send_sem, recv_sem, local_sem):
        if stage == "whole":
            list_near(own, devices, me, points_ref, ids_ref, side_ref, largest_ref)
    fetches[2].wait()


def all_gather(dims, collective_id, coords, guess, noise):
    devices = dims[0] * dims[1] * dims[2] * dims[3]
    _, own, tile = coords.shape
    wide = -(-own * CAPACITY // 128) * 128
    return pl.pallas_call(
        functools.partial(gather_kernel, dims),
        out_shape=[
            jax.ShapeDtypeStruct((devices, 4 * own, tile), jnp.float32),
            jax.ShapeDtypeStruct((devices,) + guess.shape, jnp.float32),
            jax.ShapeDtypeStruct(noise.shape, jnp.float32),
            jax.ShapeDtypeStruct((1, wide), jnp.int32),
            jax.ShapeDtypeStruct((1, wide), jnp.int32),
            jax.ShapeDtypeStruct((1,), jnp.int32),
        ],
        in_specs=[ANY_SPEC] * 3,
        out_specs=[VMEM_SPEC] * 5 + [SMEM_SPEC],
        scratch_shapes=[
            pltpu.VMEM(coords.shape, jnp.float32),
            pltpu.VMEM(guess.shape, jnp.float32),
            pltpu.VMEM((4 * own, tile), jnp.float32),
            pltpu.SemaphoreType.DMA((2 * (devices - 1),)),
            pltpu.SemaphoreType.DMA((2 * (devices - 1),)),
            pltpu.SemaphoreType.DMA((2,)),
            pltpu.SemaphoreType.DMA((3,)),
        ],
        compiler_params=pltpu.CompilerParams(collective_id=collective_id, has_side_effects=True),
    )(coords, guess, noise)


def three_parts(value):
    parts = []
    for _ in range(3):
        part = value.astype(jnp.bfloat16).astype(jnp.float32)
        parts.append(part)
        value = value - part
    return parts


def split_rows(values):
    rest = values - values.astype(jnp.bfloat16).astype(jnp.float32)
    return jnp.concatenate([values, rest], axis=0).astype(jnp.bfloat16)


def solve_kernel(
    dims, groups,
    near_ref, side_ref, points_ref, noise_ref, right_ref, guess_ref, guesses_ref,
    field_out, dir_out, residual_out, image_out, step_out,
    buffer0, buffer1, buffer2, dir_ref, blocks, own_side, centers, squared0, squared1, outgoing, dot_ref, dots_ref,
    send_sem, recv_sem, local_sem, dot_send, dot_recv,
):
    cols = dims[1] * dims[2] * dims[3]
    devices = dims[0] * cols
    own, rhs, tile = right_ref.shape
    tiles = own * devices
    me = lax.axis_index("row") * cols + lax.axis_index("col")

    def peer(k):
        number = me + k
        number = jnp.where(number >= devices, number - devices, number)
        row = lax.div(number, cols)
        return (row, number - row * cols)

    barrier = pltpu.get_barrier_semaphore()

    def greet(k, carry):
        pl.semaphore_signal(barrier, inc=1, device_id=peer(k), device_id_type=MESH)
        return carry

    lax.fori_loop(1, devices, greet, 0)

    def spreading(number, source):
        return gather(
            dims, [source], [(buffer0, buffer1, buffer2)[number]],
            send_sem.at[number], recv_sem.at[number], local_sem.at[number],
        )

    def spread(number, shadow=None):
        result = None
        for stage in spreading(number, outgoing.at[number]):
            if shadow is not None and result is None:
                result, shadow = shadow(), None
        return result

    rows = 16
    block = 2 * tile
    line = lax.broadcasted_iota(jnp.int32, (8, tile), 0)
    blank = jnp.zeros((4, tile), jnp.float32)

    def place_points(device, p):
        slab = points_ref[device]
        points = slab[:4]
        for other in range(1, own):
            points = jnp.where(p == other, slab[4 * other : 4 * other + 4], points)
        return jnp.concatenate([points, blank], axis=0)

    for p in range(own):
        points = place_points(me, p)
        center = jnp.floor(jnp.min(points, axis=1, keepdims=True))
        points = jnp.where(line < 3, points - center, 0.0)
        squares = jnp.sum(points * points, axis=0, keepdims=True)
        value = jnp.where(line == 3, 16.0, jnp.where(line == 4, 16.0 * squares, -32.0 * points))
        one, two, three = three_parts(value)
        own_side[p] = jnp.concatenate([one, two, one, three, one, two], axis=0).astype(jnp.bfloat16)
        centers[p] = jnp.broadcast_to(center, (8, tile))

    def measure(e, target):
        near = jnp.maximum(near_ref[0, e], 0)
        p = side_ref[0, e // GROUP]
        points = jnp.where(line < 3, place_points(near // own, near % own) - centers[p], 0.0)
        squares = jnp.sum(points * points, axis=0, keepdims=True)
        value = jnp.where(line == 3, squares, jnp.where(line == 4, 1.0, points))
        one, two, three = three_parts(value)
        left = jnp.concatenate([one, one, two, one, three, two], axis=0).astype(jnp.bfloat16)
        target[...] = lax.dot_general(
            left, own_side[p], (((0,), (0,)), ((), ())), preferred_element_type=jnp.float32
        )

    def weigh(e, source):
        reach = jnp.minimum(near_ref[0, e] + 1, 1).astype(jnp.float32) * 4.0
        for chunk in range(tile // rows):
            spacing = jnp.maximum(source[chunk * rows : (chunk + 1) * rows], 1e-30)
            remain = jnp.maximum(reach - spacing * lax.rsqrt(spacing), 0.0)
            twice = remain * remain
            weights = twice * twice * (5.0 - remain)
            high = weights.astype(jnp.bfloat16)
            low = (weights - high.astype(jnp.float32)).astype(jnp.bfloat16)
            at = pl.multiple_of(e * block + chunk * rows, rows)
            blocks[pl.ds(at, rows), :] = high
            at = pl.multiple_of(e * block + tile + chunk * rows, rows)
            blocks[pl.ds(at, rows), :] = low

    def build(pair, carry):
        weigh(2 * pair, squared0)
        measure(2 * pair + 1, squared1)
        weigh(2 * pair + 1, squared1)
        measure(jnp.minimum(2 * pair + 2, groups * GROUP - 1), squared0)
        return carry

    def image_of(fetch):
        def step(g, totals):
            parts = []
            for i in range(GROUP):
                near = jnp.maximum(near_ref[0, g * GROUP + i], 0)
                part = split_rows(fetch(near // own, near % own))
                parts += [part, part]
            first = pl.multiple_of(g * GROUP * block, GROUP * block)
            term = jnp.dot(
                jnp.concatenate(parts, axis=1),
                blocks[pl.ds(first, GROUP * block), :],
                preferred_element_type=jnp.float32,
            )
            place = side_ref[0, g].astype(jnp.float32)
            return tuple(
                total + term * jnp.maximum(1.0 - jnp.abs(place - float(p)), 0.0)
                for p, total in enumerate(totals)
            )

        start = tuple(jnp.zeros((2 * rhs, tile), jnp.float32) for _ in range(own))
        totals = lax.fori_loop(0, groups, step, start, unroll=8 if groups % 8 == 0 else 2)
        return [(total[:rhs] + total[rhs:]) * (1.0 / 256.0) for total in totals]

    def over_tiles(body, start):
        def one(i, carry):
            return body(i // own, i % own, carry)

        return lax.fori_loop(0, tiles, one, start, unroll=16)

    zero = jnp.zeros((rhs, tile), jnp.float32)

    def over_sums(body, count):
        start = (zero,) * count
        return [jnp.sum(total, axis=1, keepdims=True) for total in over_tiles(body, start)]

    measure(0, squared0)
    lax.fori_loop(0, groups * GROUP // 2, build, 0, unroll=4)
    noise = [noise_ref[p : p + 1, :] for p in range(own)]
    pl.semaphore_wait(barrier, devices - 1)

    for p, image in enumerate(image_of(lambda i, p: guesses_ref[i, p])):
        outgoing[0, p] = right_ref[p] - (image + noise[p] * guess_ref[p])
    spread(0)

    for p, image in enumerate(image_of(lambda i, p: buffer0[i, p])):
        outgoing[1, p] = image + noise[p] * outgoing[0, p]

    def norm_of_residual():
        def square(i, p, totals):
            value = buffer0[i, p]
            return (totals[0] + value * value,)

        return over_sums(square, 1)[0]

    norm0 = spread(1, norm_of_residual)

    for p, image in enumerate(image_of(lambda i, p: buffer1[i, p])):
        outgoing[2, p] = image + noise[p] * outgoing[1, p]

    def first_step():
        def dots(i, p, totals):
            return (totals[0] + buffer0[i, p] * buffer1[i, p],)

        step0 = norm0 / over_sums(dots, 1)[0]

        def descend(i, p, totals):
            value = buffer0[i, p] - step0 * buffer1[i, p]
            dir_ref[i, p] = value
            return (totals[0] + value * value,)

        norm1 = over_sums(descend, 1)[0]
        turn0 = norm1 / norm0

        def redirect(i, p, carry):
            value = dir_ref[i, p]
            dir_ref[i, p] = value + turn0 * buffer0[i, p]
            buffer0[i, p] = value
            return carry

        over_tiles(redirect, 0)
        return step0, norm1, turn0

    step0, norm1, turn0 = spread(2, first_step)
    grow0 = 1.0 + turn0

    def image1(i, p):
        return grow0 * buffer1[i, p] - step0 * buffer2[i, p]

    own_image1 = [grow0 * outgoing[1, p] - step0 * outgoing[2, p] for p in range(own)]
    own_residual1 = [outgoing[0, p] - step0 * outgoing[1, p] for p in range(own)]
    own_dir1 = [own_residual1[p] + turn0 * outgoing[0, p] for p in range(own)]
    images, totals = [], [zero] * 3
    for p, image in enumerate(image_of(image1)):
        image = image + noise[p] * own_image1[p]
        images.append(image)
        values = (own_residual1[p], own_image1[p], own_dir1[p])
        totals = [total + value * image for total, value in zip(totals, values)]
    lanes = lax.broadcasted_iota(jnp.int32, (rhs, 128), 1)
    eyes = [lanes == lax.broadcasted_iota(jnp.int32, (rhs, 128), 0) + n * rhs for n in range(3)]
    row = jnp.zeros((1, 128), jnp.float32)
    for eye, total in zip(eyes, totals):
        share = jnp.sum(total, axis=1, keepdims=True)
        row = row + jnp.sum(jnp.where(eye, share, 0.0), axis=0, keepdims=True)
    dot_ref[...] = row
    dots_ref[me] = row

    def dot_copy(k):
        return pltpu.make_async_remote_copy(
            src_ref=dot_ref,
            dst_ref=dots_ref.at[me],
            send_sem=dot_send.at[k],
            recv_sem=dot_recv.at[k],
            device_id=peer(k),
            device_id_type=MESH,
        )

    def start_dot(k, carry):
        dot_copy(k).start()
        return carry

    def wait_dot(k, carry):
        dot_copy(k).wait()
        return carry

    lax.fori_loop(1, devices, start_dot, 0)

    def second_dots(i, p, totals):
        direction = dir_ref[i, p]
        image = buffer1[i, p] - step0 * buffer2[i, p]
        return (
            totals[0] + direction * image1(i, p),
            totals[1] + direction * image,
        )

    dir_image1, dir_image = over_sums(second_dots, 2)
    step1 = norm1 / dir_image1

    def second_descend(i, p, totals):
        image = buffer1[i, p] - step0 * buffer2[i, p]
        turned = image1(i, p)
        value = buffer0[i, p] - step1 * turned
        return (
            totals[0] + value * value,
            totals[1] + value * image,
            totals[2] + value * turned,
        )

    norm2, next_image, next_image1 = over_sums(second_descend, 3)
    turn1 = norm2 / norm1
    known = next_image + turn1 * (next_image1 + dir_image + turn1 * dir_image1)
    for p in range(own):
        residual = own_residual1[p] - step1 * own_image1[p]
        field_out[p] = guess_ref[p] + step0 * outgoing[0, p] + step1 * own_dir1[p]
        residual_out[p] = residual
        dir_out[p] = residual + turn1 * own_dir1[p]
        image_out[p] = (
            outgoing[1, p] - step0 * outgoing[2, p] - step1 * images[p] + turn1 * own_image1[p]
        )

    lax.fori_loop(1, devices, wait_dot, 0)
    sums = jnp.sum(dots_ref[...], axis=0)
    first, second, third = [
        jnp.sum(jnp.where(eye, sums, 0.0), axis=1, keepdims=True) for eye in eyes
    ]
    step2 = norm2 / (known - step1 * (first - step1 * second + turn1 * third))
    step_out[...] = jnp.broadcast_to(step2, (rhs, tile))


def solve(dims, groups, collective_id, *operands):
    devices = dims[0] * dims[1] * dims[2] * dims[3]
    right = operands[4]
    own, rhs, tile = right.shape
    dma = pltpu.SemaphoreType.DMA
    phases = ITERS
    return pl.pallas_call(
        functools.partial(solve_kernel, dims, groups),
        out_shape=[jax.ShapeDtypeStruct(right.shape, jnp.float32)] * 4
        + [jax.ShapeDtypeStruct((rhs, tile), jnp.float32)],
        in_specs=[SMEM_SPEC] * 2 + [VMEM_SPEC] * 5,
        out_specs=[VMEM_SPEC] * 5,
        scratch_shapes=[
            *[pltpu.VMEM((devices, own, rhs, tile), jnp.float32)] * (phases + 1),
            pltpu.VMEM((groups * GROUP * 2 * tile, tile), jnp.bfloat16),
            pltpu.VMEM((own, 48, tile), jnp.bfloat16),
            pltpu.VMEM((own, 8, tile), jnp.float32),
            *[pltpu.VMEM((tile, tile), jnp.float32)] * 2,
            pltpu.VMEM((ITERS, own, rhs, tile), jnp.float32),
            pltpu.VMEM((1, 128), jnp.float32),
            pltpu.VMEM((devices, 1, 128), jnp.float32),
            dma((phases, devices - 1)),
            dma((phases, devices - 1)),
            dma((phases, 1)),
            dma((devices,)),
            dma((devices,)),
        ],
        compiler_params=pltpu.CompilerParams(
            collective_id=collective_id, has_side_effects=True, vmem_limit_bytes=60 * 2**20
        ),
    )(*operands)


def shards(mesh_shape, coords, noise_var, right_side, start_guess, tile_pairs):
    dims = factors(mesh_shape)
    own = coords.shape[0]
    placed = jnp.transpose(coords, (1, 0, 2))
    gathered = all_gather(dims, 0, placed, start_guess, noise_var)
    points, guesses, noise, near_ids, side, largest = gathered
    operands = (near_ids, side, points, noise, right_side, start_guess, guesses)
    small = own * 4
    field, direction, residual, image, step = lax.cond(
        largest[0] <= small,
        functools.partial(solve, dims, small, 1),
        functools.partial(solve, dims, own * CAPACITY // GROUP, 2),
        *operands,
    )
    return field + step * direction, residual - step * image


def solution(mesh):
    placed = (
        P(("row", "col"), None, None),
        P(("row", "col"), None),
        P(("row", "col"), None, None),
        P(("row", "col"), None, None),
        P("row", "col", None, None),
    )
    return jax.shard_map(
        functools.partial(shards, (mesh.shape["row"], mesh.shape["col"])),
        mesh=mesh,
        in_specs=placed,
        out_specs=(P(("row", "col"), None, None), P(("row", "col"), None, None)),
        check_vma=False,
    )
```

```python
import functools

import jax
import jax.numpy as jnp
from jax import lax
from jax.experimental import pallas as pl
from jax.experimental.pallas import tpu as pltpu
from jax.sharding import PartitionSpec as P

ITERS = 3
GROUP = 3
NEAR = 27
CAPACITY = -(-NEAR // GROUP) * GROUP
CORES = 2
MESH = pl.DeviceIdType.MESH
VMEM_SPEC = pl.BlockSpec(memory_space=pltpu.VMEM)
SMEM_SPEC = pl.BlockSpec(memory_space=pltpu.SMEM)
ANY_SPEC = pl.BlockSpec(memory_space=pl.ANY)


def factors(mesh_shape):
    rows, cols = mesh_shape
    chips = cols // CORES
    wide = 1
    while wide * wide * 4 <= chips:
        wide *= 2
    return rows, chips // wide, wide, CORES


def position(dims):
    xs, zs, ys, cs = dims
    x = lax.axis_index("row")
    col = lax.axis_index("col")
    return x, col // (ys * cs), (col // cs) % ys, col % cs


def flip(index, k, size):
    if size & (size - 1):
        return (k - index + 2 * size) % size
    result, bit = 0, 1
    while bit < size:
        result = result + (index // bit + k // bit) % 2 * bit
        bit *= 2
    return result


def plane_order(x, y, c):
    return (1 - x, 1 - y), ((x + c) % 2, (y + 1 - c) % 2), ((x + 1 - c) % 2, (y + c) % 2)


def straight(k, levels, arrays):
    if arrays > 1 or k == 0 or k + 1 >= levels:
        return ()
    return (0, 1, 2)[: 3 if k == 1 else 1 if k == 2 else 0]


def gather_partners(dims):
    xs, zs, ys, cs = dims
    x, z, y, c = position(dims)
    partners = [(x, (((z + k) % zs) * ys + y) * cs + c) for k in range(1, zs)]
    if xs == 2 and ys == 2:
        partners += [(1 - x, (z * ys + 1 - y) * cs + c)]
        partners += [(1 - x, (z * ys + yy) * cs + 1 - c) for yy in range(ys)]
        partners += [(x, (z * ys + 1 - y) * cs + 1 - c)]
    partners += [(x, (z * ys + (y + k) % ys) * cs + c) for k in range(1, ys)]
    partners += [((x + k) % xs, (z * ys + y) * cs + c) for k in range(1, xs)]
    partners += [(x, (z * ys + y) * cs + 1 - c)]
    return partners


def gather(dims, ins, outs, send_sem, recv_sem, local_sem):
    xs, zs, ys, cs = dims
    count = len(ins)
    x, z, y, c = position(dims)

    def device(xx, zz, yy, cc):
        return (xx, (zz * ys + yy) * cs + cc)

    def slot(xx, zz, yy, cc):
        return ((xx * zs + zz) * ys + yy) * cs + cc

    local = []
    for a in range(count):
        copy = pltpu.make_async_copy(ins[a], outs[a].at[slot(x, z, y, c)], local_sem.at[a])
        copy.start()
        local.append(copy)

    numbers = iter(range(10**6))
    sent = []

    def send(a, source, place, target):
        number = next(numbers)
        copy = pltpu.make_async_remote_copy(
            src_ref=source,
            dst_ref=outs[a].at[place],
            send_sem=send_sem.at[number],
            recv_sem=recv_sem.at[number],
            device_id=target,
            device_id_type=MESH,
        )
        copy.start()
        sent.append(copy)
        return copy

    mine = slot(x, z, y, c)
    other = device(x, z, y, 1 - c)
    along_z = {}
    if xs == 2 and ys == 2:
        across_by = plane_order(x, y, c)
        last = zs - 1
        arrivals, swaps = {}, []

        def hand_on(k, a):
            level = flip(z, k, zs)
            if k:
                along_z[k, a].wait_recv()
            place = slot(x, level, y, c)
            source = outs[a].at[place] if k else ins[a]
            for way, (xx, yy) in enumerate(across_by):
                if way in straight(k, zs, count):
                    continue
                copy = send(a, source, place, device(xx, z, yy, c))
                arrivals[a, k, way] = (copy, slot(xx, level, yy, c))
                if k and k == last:
                    swaps.append((a, send(a, source, place, device(xx, z, yy, 1 - c))))
            swaps.append((a, send(a, source, place, other)))

        for k in reversed(range(1, zs)):
            for a in range(count):
                level = flip(z, k, zs)
                if k > 1:
                    along_z[k, a] = send(a, ins[a], mine, device(x, level, y, c))
                for way in straight(k, zs, count):
                    xx, yy = across_by[way]
                    copy = send(a, ins[a], mine, device(xx, level, yy, c))
                    arrivals[a, k, way] = (copy, slot(xx, level, yy, c))
                if k == 1:
                    along_z[k, a] = send(a, ins[a], mine, device(x, level, y, c))
        for a in range(count):
            hand_on(0, a)
        yield "sent"
        for k in sorted(range(1, zs), key=lambda k: (len(straight(k, zs, count)) == 3, k)):
            for a in range(count):
                hand_on(k, a)
        ways = (1, 2, 0)
        early = min(zs, 2) if count == 1 else 0
        order = [(k, way) for k in range(early) for way in ways]
        order += [(k, way) for way in ways for k in range(early, zs)]
        order.sort(key=lambda step: step[0] == last)
        for first in range(count):
            for k, way in order:
                copy, place = arrivals[first, k, way]
                copy.wait_recv()
                if k == 0 or k < last:
                    swaps.append((first, send(first, outs[first].at[place], place, other)))
        for first in range(count):
            for a, copy in swaps:
                if a == first:
                    copy.wait_recv()
            local[first].wait()
            if first == 0:
                yield "whole"
        for copy in sent:
            copy.wait_send()
        return

    for k in reversed(range(1, zs)):
        for a in range(count):
            along_z[k, a] = send(a, ins[a], mine, device(x, flip(z, k, zs), y, c))
    for copy in local:
        copy.wait()

    def across(places, targets):
        for place in places:
            for a in range(count):
                for target in targets:
                    send(a, outs[a].at[place], place, target)

    def settle():
        for copy in sent:
            copy.wait()
        del sent[:]

    settle()
    across(
        [slot(x, zz, y, c) for zz in range(zs)],
        [device(x, z, (y + k) % ys, c) for k in range(1, ys)],
    )
    settle()
    across(
        [slot(x, zz, yy, c) for zz in range(zs) for yy in range(ys)],
        [device((x + k) % xs, z, y, c) for k in range(1, xs)],
    )
    settle()
    across(
        [slot(xx, zz, yy, c) for xx in range(xs) for zz in range(zs) for yy in range(ys)],
        [other],
    )
    settle()
    yield "whole"


def column_of(matrix, lane):
    lanes = lax.broadcasted_iota(jnp.int32, matrix.shape, 1)
    return jnp.sum(jnp.where(lanes == lane, matrix, 0.0), axis=1, keepdims=True)


def list_near(own, devices, me, points_ref, ids_ref, side_ref, largest_ref):
    tiles = own * devices
    table = jnp.concatenate([points_ref[:, 4 * p + 3, :128] for p in range(own)], axis=0)
    across = table.T
    far = None
    for component in range(3):
        low, high = table[:, component : component + 1], table[:, component + 3 : component + 4]
        low_row, high_row = across[component : component + 1], across[component + 3 : component + 4]
        gap = jnp.maximum(low - high_row, low_row - high)
        far = gap if far is None else jnp.maximum(far, gap)
    near = jnp.where(far < 1.0, 1.0, 0.0)
    needed = jnp.ceil((jnp.sum(near, axis=1, keepdims=True) - 0.5) * (1.0 / GROUP))
    groups = sum(needed[p * devices : (p + 1) * devices] for p in range(own))
    largest_ref[0] = jnp.max(groups).astype(jnp.int32)

    rows = lax.broadcasted_iota(jnp.int32, (tiles, tiles), 0)
    earlier = rows > lax.broadcasted_iota(jnp.int32, (tiles, tiles), 1)
    rank = jnp.dot(
        jnp.where(earlier, 1.0, 0.0).astype(jnp.bfloat16),
        near.astype(jnp.bfloat16),
        preferred_element_type=jnp.float32,
    )
    slots = lax.broadcasted_iota(jnp.int32, (tiles, ids_ref.shape[1]), 1).astype(jnp.float32)
    place = lax.broadcasted_iota(jnp.int32, (tiles, 1), 0)
    tile_ids = (place % devices * own + place // devices + 1).astype(jnp.float32)
    slot_ids = lax.broadcasted_iota(jnp.int32, side_ref.shape, 1).astype(jnp.float32)
    found, side = 0.0, jnp.zeros(side_ref.shape, jnp.float32)
    first = jnp.zeros((1, 1), jnp.float32)
    for p in range(own):
        lane = p * devices + me
        chosen = column_of(near, lane)
        goal = jnp.where(chosen > 0.0, column_of(rank, lane) + first * GROUP, -1.0)
        found = found + jnp.where(goal == slots, tile_ids, 0.0)
        if p:
            side = side + jnp.where(slot_ids >= first * GROUP, 1.0, 0.0)
        first = first + jnp.ceil((jnp.sum(chosen, axis=0, keepdims=True) - 0.5) * (1.0 / GROUP))
    ids_ref[...] = (jnp.sum(found, axis=0, keepdims=True) - 1.0).astype(jnp.int32)
    side_ref[...] = side.astype(jnp.int32)


def gather_kernel(dims, coords_in, guess_in, noise_in, points_ref, guesses_ref, noise_out, ids_ref, side_ref,
                  largest_ref, coords_ref, guess_ref, slab_ref, send_sem, recv_sem,
                  local_sem, fetch_sem):
    own = coords_ref.shape[1]
    cols = dims[1] * dims[2] * dims[3]
    devices = dims[0] * cols
    fetches = [
        pltpu.make_async_copy(coords_in, coords_ref, fetch_sem.at[0]),
        pltpu.make_async_copy(guess_in, guess_ref, fetch_sem.at[1]),
        pltpu.make_async_copy(noise_in, noise_out, fetch_sem.at[2]),
    ]
    for fetch in fetches:
        fetch.start()
    partners = gather_partners(dims)
    barrier = pltpu.get_barrier_semaphore()
    for partner in partners:
        pl.semaphore_signal(barrier, inc=1, device_id=partner, device_id_type=MESH)
    fetches[0].wait()
    lanes = lax.broadcasted_iota(jnp.int32, (1, coords_ref.shape[2]), 1)
    for p in range(own):
        box = jnp.zeros(lanes.shape, jnp.float32)
        for component in range(3):
            row = coords_ref[component, p : p + 1, :]
            slab_ref[4 * p + component : 4 * p + component + 1, :] = row
            box = jnp.where(lanes == component, jnp.min(row, axis=1, keepdims=True), box)
            box = jnp.where(lanes == component + 3, jnp.max(row, axis=1, keepdims=True), box)
        slab_ref[4 * p + 3 : 4 * p + 4, :] = box
    fetches[1].wait()
    pl.semaphore_wait(barrier, len(partners))
    ins, outs = [slab_ref, guess_ref], [points_ref, guesses_ref]
    me = lax.axis_index("row") * cols + lax.axis_index("col")
    for stage in gather(dims, ins, outs, send_sem, recv_sem, local_sem):
        if stage == "whole":
            list_near(own, devices, me, points_ref, ids_ref, side_ref, largest_ref)
    fetches[2].wait()


def all_gather(dims, collective_id, coords, guess, noise):
    devices = dims[0] * dims[1] * dims[2] * dims[3]
    _, own, tile = coords.shape
    wide = -(-own * CAPACITY // 128) * 128
    return pl.pallas_call(
        functools.partial(gather_kernel, dims),
        out_shape=[
            jax.ShapeDtypeStruct((devices, 4 * own, tile), jnp.float32),
            jax.ShapeDtypeStruct((devices,) + guess.shape, jnp.float32),
            jax.ShapeDtypeStruct(noise.shape, jnp.float32),
            jax.ShapeDtypeStruct((1, wide), jnp.int32),
            jax.ShapeDtypeStruct((1, wide), jnp.int32),
            jax.ShapeDtypeStruct((1,), jnp.int32),
        ],
        in_specs=[ANY_SPEC] * 3,
        out_specs=[VMEM_SPEC] * 5 + [SMEM_SPEC],
        scratch_shapes=[
            pltpu.VMEM(coords.shape, jnp.float32),
            pltpu.VMEM(guess.shape, jnp.float32),
            pltpu.VMEM((4 * own, tile), jnp.float32),
            pltpu.SemaphoreType.DMA((2 * (devices - 1),)),
            pltpu.SemaphoreType.DMA((2 * (devices - 1),)),
            pltpu.SemaphoreType.DMA((2,)),
            pltpu.SemaphoreType.DMA((3,)),
        ],
        compiler_params=pltpu.CompilerParams(collective_id=collective_id, has_side_effects=True),
    )(coords, guess, noise)


def three_parts(value):
    parts = []
    for _ in range(3):
        part = value.astype(jnp.bfloat16).astype(jnp.float32)
        parts.append(part)
        value = value - part
    return parts


def split_rows(values):
    rest = values - values.astype(jnp.bfloat16).astype(jnp.float32)
    return jnp.concatenate([values, rest], axis=0).astype(jnp.bfloat16)


def solve_kernel(
    dims, groups,
    near_ref, side_ref, points_ref, noise_ref, right_ref, guess_ref, guesses_ref,
    field_out, dir_out, residual_out, image_out, step_out,
    buffer0, buffer1, buffer2, dir_ref, blocks, own_side, centers, squared0, squared1, outgoing, dot_ref, dots_ref,
    send_sem, recv_sem, local_sem, dot_send, dot_recv,
):
    cols = dims[1] * dims[2] * dims[3]
    devices = dims[0] * cols
    own, rhs, tile = right_ref.shape
    tiles = own * devices
    me = lax.axis_index("row") * cols + lax.axis_index("col")

    def peer(k):
        number = me + k
        number = jnp.where(number >= devices, number - devices, number)
        row = lax.div(number, cols)
        return (row, number - row * cols)

    barrier = pltpu.get_barrier_semaphore()

    def greet(k, carry):
        pl.semaphore_signal(barrier, inc=1, device_id=peer(k), device_id_type=MESH)
        return carry

    lax.fori_loop(1, devices, greet, 0)

    def spreading(number, source):
        return gather(
            dims, [source], [(buffer0, buffer1, buffer2)[number]],
            send_sem.at[number], recv_sem.at[number], local_sem.at[number],
        )

    def spread(number, shadow=None):
        result = None
        for stage in spreading(number, outgoing.at[number]):
            if shadow is not None and result is None:
                result, shadow = shadow(), None
        return result

    rows = 16
    block = 2 * tile
    line = lax.broadcasted_iota(jnp.int32, (8, tile), 0)
    blank = jnp.zeros((4, tile), jnp.float32)

    def place_points(device, p):
        slab = points_ref[device]
        points = slab[:4]
        for other in range(1, own):
            points = jnp.where(p == other, slab[4 * other : 4 * other + 4], points)
        return jnp.concatenate([points, blank], axis=0)

    for p in range(own):
        points = place_points(me, p)
        center = jnp.floor(jnp.min(points, axis=1, keepdims=True))
        points = jnp.where(line < 3, points - center, 0.0)
        squares = jnp.sum(points * points, axis=0, keepdims=True)
        value = jnp.where(line == 3, 16.0, jnp.where(line == 4, 16.0 * squares, -32.0 * points))
        one, two, three = three_parts(value)
        own_side[p] = jnp.concatenate([one, two, one, three, one, two], axis=0).astype(jnp.bfloat16)
        centers[p] = jnp.broadcast_to(center, (8, tile))

    def measure(e, target):
        near = jnp.maximum(near_ref[0, e], 0)
        p = side_ref[0, e]
        points = jnp.where(line < 3, place_points(near // own, near % own) - centers[p], 0.0)
        squares = jnp.sum(points * points, axis=0, keepdims=True)
        value = jnp.where(line == 3, squares, jnp.where(line == 4, 1.0, points))
        one, two, three = three_parts(value)
        left = jnp.concatenate([one, one, two, one, three, two], axis=0).astype(jnp.bfloat16)
        target[...] = lax.dot_general(
            left, own_side[p], (((0,), (0,)), ((), ())), preferred_element_type=jnp.float32
        )

    def weigh(e, source):
        reach = jnp.minimum(near_ref[0, e] + 1, 1).astype(jnp.float32) * 4.0
        for chunk in range(tile // rows):
            spacing = jnp.maximum(source[chunk * rows : (chunk + 1) * rows], 1e-30)
            remain = jnp.maximum(reach - spacing * lax.rsqrt(spacing), 0.0)
            twice = remain * remain
            weights = twice * twice * (5.0 - remain)
            high = weights.astype(jnp.bfloat16)
            low = (weights - high.astype(jnp.float32)).astype(jnp.bfloat16)
            at = pl.multiple_of(e * block + chunk * rows, rows)
            blocks[pl.ds(at, rows), :] = high
            at = pl.multiple_of(e * block + tile + chunk * rows, rows)
            blocks[pl.ds(at, rows), :] = low

    def build(pair, carry):
        weigh(2 * pair, squared0)
        measure(2 * pair + 1, squared1)
        weigh(2 * pair + 1, squared1)
        measure(jnp.minimum(2 * pair + 2, groups * GROUP - 1), squared0)
        return carry

    def image_of(fetch):
        def step(g, totals):
            parts = []
            for i in range(GROUP):
                near = jnp.maximum(near_ref[0, g * GROUP + i], 0)
                part = split_rows(fetch(near // own, near % own))
                parts += [part, part]
            first = pl.multiple_of(g * GROUP * block, GROUP * block)
            term = jnp.dot(
                jnp.concatenate(parts, axis=1),
                blocks[pl.ds(first, GROUP * block), :],
                preferred_element_type=jnp.float32,
            )
            place = side_ref[0, g * GROUP].astype(jnp.float32)
            return tuple(
                total + term * jnp.maximum(1.0 - jnp.abs(place - float(p)), 0.0)
                for p, total in enumerate(totals)
            )

        start = tuple(jnp.zeros((2 * rhs, tile), jnp.float32) for _ in range(own))
        totals = lax.fori_loop(0, groups, step, start, unroll=10 if groups % 10 == 0 else 2)
        return [(total[:rhs] + total[rhs:]) * (1.0 / 256.0) for total in totals]

    def over_tiles(body, start):
        def one(i, carry):
            return body(i // own, i % own, carry)

        return lax.fori_loop(0, tiles, one, start, unroll=16)

    zero = jnp.zeros((rhs, tile), jnp.float32)

    def over_sums(body, count):
        start = (zero,) * count
        return [jnp.sum(total, axis=1, keepdims=True) for total in over_tiles(body, start)]

    measure(0, squared0)
    lax.fori_loop(0, groups * GROUP // 2, build, 0, unroll=5 if groups % 5 == 0 else 1)
    noise = [noise_ref[p : p + 1, :] for p in range(own)]
    pl.semaphore_wait(barrier, devices - 1)

    for p, image in enumerate(image_of(lambda i, p: guesses_ref[i, p])):
        outgoing[0, p] = right_ref[p] - (image + noise[p] * guess_ref[p])
    spread(0)

    for p, image in enumerate(image_of(lambda i, p: buffer0[i, p])):
        outgoing[1, p] = image + noise[p] * outgoing[0, p]

    def norm_of_residual():
        def square(i, p, totals):
            value = buffer0[i, p]
            return (totals[0] + value * value,)

        return over_sums(square, 1)[0]

    norm0 = spread(1, norm_of_residual)

    for p, image in enumerate(image_of(lambda i, p: buffer1[i, p])):
        outgoing[2, p] = image + noise[p] * outgoing[1, p]

    def first_step():
        def dots(i, p, totals):
            return (totals[0] + buffer0[i, p] * buffer1[i, p],)

        step0 = norm0 / over_sums(dots, 1)[0]

        def descend(i, p, totals):
            value = buffer0[i, p] - step0 * buffer1[i, p]
            dir_ref[i, p] = value
            return (totals[0] + value * value,)

        norm1 = over_sums(descend, 1)[0]
        turn0 = norm1 / norm0

        def redirect(i, p, carry):
            value = dir_ref[i, p]
            dir_ref[i, p] = value + turn0 * buffer0[i, p]
            buffer0[i, p] = value
            return carry

        over_tiles(redirect, 0)
        return step0, norm1, turn0

    step0, norm1, turn0 = spread(2, first_step)
    grow0 = 1.0 + turn0

    def image1(i, p):
        return grow0 * buffer1[i, p] - step0 * buffer2[i, p]

    own_image1 = [grow0 * outgoing[1, p] - step0 * outgoing[2, p] for p in range(own)]
    own_residual1 = [outgoing[0, p] - step0 * outgoing[1, p] for p in range(own)]
    own_dir1 = [own_residual1[p] + turn0 * outgoing[0, p] for p in range(own)]
    images, totals = [], [zero] * 3
    for p, image in enumerate(image_of(image1)):
        image = image + noise[p] * own_image1[p]
        images.append(image)
        values = (own_residual1[p], own_image1[p], own_dir1[p])
        totals = [total + value * image for total, value in zip(totals, values)]
    lanes = lax.broadcasted_iota(jnp.int32, (rhs, 128), 1)
    eyes = [lanes == lax.broadcasted_iota(jnp.int32, (rhs, 128), 0) + n * rhs for n in range(3)]
    row = jnp.zeros((1, 128), jnp.float32)
    for eye, total in zip(eyes, totals):
        share = jnp.sum(total, axis=1, keepdims=True)
        row = row + jnp.sum(jnp.where(eye, share, 0.0), axis=0, keepdims=True)
    dot_ref[...] = row
    dots_ref[me] = row

    def dot_copy(k):
        return pltpu.make_async_remote_copy(
            src_ref=dot_ref,
            dst_ref=dots_ref.at[me],
            send_sem=dot_send.at[k],
            recv_sem=dot_recv.at[k],
            device_id=peer(k),
            device_id_type=MESH,
        )

    def start_dot(k, carry):
        dot_copy(k).start()
        return carry

    def wait_dot(k, carry):
        dot_copy(k).wait()
        return carry

    lax.fori_loop(1, devices, start_dot, 0)

    def second_dots(i, p, totals):
        direction = dir_ref[i, p]
        image = buffer1[i, p] - step0 * buffer2[i, p]
        return (
            totals[0] + direction * image1(i, p),
            totals[1] + direction * image,
        )

    dir_image1, dir_image = over_sums(second_dots, 2)
    step1 = norm1 / dir_image1

    def second_descend(i, p, totals):
        image = buffer1[i, p] - step0 * buffer2[i, p]
        turned = image1(i, p)
        value = buffer0[i, p] - step1 * turned
        return (
            totals[0] + value * value,
            totals[1] + value * image,
            totals[2] + value * turned,
        )

    norm2, next_image, next_image1 = over_sums(second_descend, 3)
    turn1 = norm2 / norm1
    known = next_image + turn1 * (next_image1 + dir_image + turn1 * dir_image1)
    for p in range(own):
        residual = own_residual1[p] - step1 * own_image1[p]
        field_out[p] = guess_ref[p] + step0 * outgoing[0, p] + step1 * own_dir1[p]
        residual_out[p] = residual
        dir_out[p] = residual + turn1 * own_dir1[p]
        image_out[p] = (
            outgoing[1, p] - step0 * outgoing[2, p] - step1 * images[p] + turn1 * own_image1[p]
        )

    lax.fori_loop(1, devices, wait_dot, 0)
    sums = jnp.sum(dots_ref[...], axis=0)
    first, second, third = [
        jnp.sum(jnp.where(eye, sums, 0.0), axis=1, keepdims=True) for eye in eyes
    ]
    step2 = norm2 / (known - step1 * (first - step1 * second + turn1 * third))
    step_out[...] = jnp.broadcast_to(step2, (rhs, tile))


def solve(dims, groups, collective_id, *operands):
    devices = dims[0] * dims[1] * dims[2] * dims[3]
    right = operands[4]
    own, rhs, tile = right.shape
    dma = pltpu.SemaphoreType.DMA
    phases = ITERS
    return pl.pallas_call(
        functools.partial(solve_kernel, dims, groups),
        out_shape=[jax.ShapeDtypeStruct(right.shape, jnp.float32)] * 4
        + [jax.ShapeDtypeStruct((rhs, tile), jnp.float32)],
        in_specs=[SMEM_SPEC] * 2 + [VMEM_SPEC] * 5,
        out_specs=[VMEM_SPEC] * 5,
        scratch_shapes=[
            *[pltpu.VMEM((devices, own, rhs, tile), jnp.float32)] * (phases + 1),
            pltpu.VMEM((groups * GROUP * 2 * tile, tile), jnp.bfloat16),
            pltpu.VMEM((own, 48, tile), jnp.bfloat16),
            pltpu.VMEM((own, 8, tile), jnp.float32),
            *[pltpu.VMEM((tile, tile), jnp.float32)] * 2,
            pltpu.VMEM((ITERS, own, rhs, tile), jnp.float32),
            pltpu.VMEM((1, 128), jnp.float32),
            pltpu.VMEM((devices, 1, 128), jnp.float32),
            dma((phases, devices - 1)),
            dma((phases, devices - 1)),
            dma((phases, 1)),
            dma((devices,)),
            dma((devices,)),
        ],
        compiler_params=pltpu.CompilerParams(
            collective_id=collective_id, has_side_effects=True, vmem_limit_bytes=60 * 2**20
        ),
    )(*operands)


def shards(mesh_shape, coords, noise_var, right_side, start_guess, tile_pairs):
    dims = factors(mesh_shape)
    own = coords.shape[0]
    placed = jnp.transpose(coords, (1, 0, 2))
    gathered = all_gather(dims, 0, placed, start_guess, noise_var)
    points, guesses, noise, near_ids, side, largest = gathered
    operands = (near_ids, side, points, noise, right_side, start_guess, guesses)
    small = own * 5
    field, direction, residual, image, step = lax.cond(
        largest[0] <= small,
        functools.partial(solve, dims, small, 1),
        functools.partial(solve, dims, own * CAPACITY // GROUP, 2),
        *operands,
    )
    return field + step * direction, residual - step * image


def solution(mesh):
    placed = (
        P(("row", "col"), None, None),
        P(("row", "col"), None),
        P(("row", "col"), None, None),
        P(("row", "col"), None, None),
        P("row", "col", None, None),
    )
    return jax.shard_map(
        functools.partial(shards, (mesh.shape["row"], mesh.shape["col"])),
        mesh=mesh,
        in_specs=placed,
        out_specs=(P(("row", "col"), None, None), P(("row", "col"), None, None)),
        check_vma=False,
    )
```
